256 devices in a mesh: rep: 64 (over z, x, core), tp: 4 (over y).
Axes of the slice: x: 4, y: 4, z: 8, core: 2. Of those that a mesh axis runs over, the one named last changes fastest.
Arguments:
- suffix_source: bfloat16 [64, 384, 4096], P('rep', None, 'tp'), may hold values from -6 to 6
- suffix_accept: bfloat16 [64, 384, 4096], P('rep', None, 'tp'), may hold values from -3 to 3
- suffix_address: bfloat16 [64, 384, 4096], P('rep', None, 'tp'), may hold values from -3 to 3
- guess_lane_source: bfloat16 [128, 16, 4096], P('rep', None, 'tp'), may hold values from -6 to 6
- guess_lane_accept: bfloat16 [128, 16, 4096], P('rep', None, 'tp'), may hold values from -3 to 3
- guess_lane_address: bfloat16 [128, 16, 4096], P('rep', None, 'tp'), may hold values from -3 to 3
- content_map: bfloat16 [4096, 4096], P(None, 'tp'), may hold values from -0.09375 to 0.09375
- forget_shrink_map: bfloat16 [4096, 128], replicated, may hold values from -0.09375 to 0.09375
- forget_expand_map: bfloat16 [128, 4096], P(None, 'tp'), may hold values from -0.35351562 to 0.35351562
- forget_lane_anchor: float32 [4096], P('tp'), may hold values from -12 to -3
- present_boost: float32 [4096], P('tp'), may hold values from -1.5 to 1.5
- content_blend_share: float32 [4096], P('tp'), may hold values from 0 to 1
- forget_blend_share: float32 [4096], P('tp'), may hold values from 0 to 1
- lane_normal_scale: float32 [4096], P('tp'), may hold values from 0.5 to 1.5
- lane_normal_shift: float32 [4096], P('tp'), may hold values from -1.2 to 1.2
- kernel_memory_saved: float32 [128, 64, 4096], P(None, 'rep', 'tp'), may hold values from -6 to 6
- prior_source_saved: bfloat16 [128, 64, 64], P(None, 'rep', 'tp'), may hold values from -6 to 6
- lane_owner: int32 [128], replicated, may hold values from 0 to 127, as said below
- request_spans: int32 [128], replicated, may hold values from 16 to 400, as said below
- admitted_guesses: int32 [128], replicated, may hold values from 0 to 16
Outputs:
- tail_out: bfloat16 [64, 384, 4096], P('rep', None, 'tp')
- draft_out: bfloat16 [128, 16, 4096], P('rep', None, 'tp')
- state_out: float32 [128, 64, 4096], P(None, 'rep', 'tp')
- shift_out: bfloat16 [128, 64, 64], P(None, 'rep', 'tp')
The draws below stay inside these ranges and needn't reach their ends.
Inputs may be any that keep to these rules, and one draw needn't show every extreme that they name: `lane_owner`: a permutation of the request numbers. `request_spans`: exactly 8 requests have 16 + 384 tokens and the others 16; a long request is always dealt to a slot s with s % 2 == 0; each aligned block of 8 consecutive groups holds exactly one group whose first slot is long; the tail buffers of groups whose first slot is not long are not read.
All inputs are finite; a program needn't handle non-finite values.
Results may differ from the reference program's by a relative error of at most 0.0051.
The reference program's roundings to bfloat16 on the way count: a program that leaves them out, or rounds other values in their place, can miss the bound.
Values may be sent and summed in bfloat16 or wider, within the bound.
A program may use at most 128 MiB of HBM per device.

```python
import math
import jax
import jax.numpy as jnp
from jax import lax

HIDDEN_BREADTH = 4096
BLEND_LANES = 64
SUBSPACE_SPAN = 64
DECAY_RANK = 128
DRAFT = 16
TAIL = 384
REQ_DEV = 2
GROUPS = 64
REQS = 128
LONGS = 8


def dealing(key):
    order_req = jax.random.permutation(jax.random.fold_in(key, 11), REQS).astype(jnp.int32)
    offsets = jax.random.randint(jax.random.fold_in(key, 12), (LONGS,), 0, 8, jnp.int32)
    chosen = jnp.arange(LONGS, dtype=jnp.int32) * 8 + offsets
    long_reqs = order_req[chosen * REQ_DEV]
    length_table = jnp.full((REQS,), DRAFT, jnp.int32).at[long_reqs].set(DRAFT + TAIL)
    return (order_req, length_table)


def draw_lane_owner(key, part):
    return dealing(key)[0]


def draw_request_spans(key, part):
    return dealing(key)[1]


def draw_forget_lane_anchor(key, part):
    chain = TAIL + DRAFT
    head_key = jax.random.fold_in(key, 21)
    chan_key = jax.random.fold_in(key, 22)
    place = jax.random.uniform(head_key, (BLEND_LANES, 1), jnp.float32)
    noise = jax.random.uniform(chan_key, (BLEND_LANES, SUBSPACE_SPAN), jnp.float32, -0.5, 0.5)
    base = math.log(1.0 / 40.0) + place * math.log(40.0 / (8.0 * chain))
    return (base + noise).reshape(HIDDEN_BREADTH)


def touch_ends(entries, rng, smallest, largest):
    index_at = [jax.random.randint(jax.random.fold_in(rng, axis), (), 0, length) for axis, length in enumerate(entries.shape)]
    main_axis = entries.shape.index(max(entries.shape))
    beside = index_at[:main_axis] + [(index_at[main_axis] + 1) % entries.shape[main_axis]] + index_at[main_axis + 1:]
    return entries.at[tuple(index_at)].set(smallest).at[tuple(beside)].set(largest)


def block_scale(rng, extent, split, low, top_value):
    factor_of = 1.0
    for position, parts in split:
        steps = jax.random.uniform(jax.random.fold_in(jax.random.fold_in(rng, 6), position), (parts,), jnp.float32, low / len(split), top_value / len(split))
        factor_of = factor_of * jnp.repeat(jnp.exp(steps), extent[position] // parts).reshape((-1,) + (1,) * (len(extent) - 1 - position))
    return factor_of


def centred(own_key, dims, deviation, limit, cuts=(), held_as=jnp.bfloat16):
    factor_of = block_scale(own_key, dims, cuts, -0.22, 0.18) if cuts else 1.0
    drawn = jax.random.normal(own_key, dims, jnp.float32) * deviation * factor_of
    return jnp.minimum(jnp.maximum(drawn, -limit), limit).astype(held_as)


def setup_inputs(seed: int = 0) -> dict:
    splits = jax.random.split(jax.random.key(seed), 21)
    suffix_source = centred(splits[0], (GROUPS, TAIL, HIDDEN_BREADTH), 1.0, 6.0, ((0, 64), (2, 4)))
    suffix_accept = centred(splits[1], (GROUPS, TAIL, HIDDEN_BREADTH), 0.5, 3.0, ((0, 64), (2, 4)))
    suffix_address = centred(splits[2], (GROUPS, TAIL, HIDDEN_BREADTH), 0.5, 3.0, ((0, 64), (2, 4)))
    guess_lane_source = centred(splits[3], (REQS, DRAFT, HIDDEN_BREADTH), 1.0, 6.0, ((0, 64), (2, 4)))
    guess_lane_accept = centred(splits[4], (REQS, DRAFT, HIDDEN_BREADTH), 0.5, 3.0, ((0, 64), (2, 4)))
    guess_lane_address = centred(splits[5], (REQS, DRAFT, HIDDEN_BREADTH), 0.5, 3.0, ((0, 64), (2, 4)))
    content_map = centred(splits[6], (HIDDEN_BREADTH, HIDDEN_BREADTH), HIDDEN_BREADTH ** -0.5, 0.09375, ((1, 4),))
    forget_shrink_map = centred(splits[7], (HIDDEN_BREADTH, DECAY_RANK), HIDDEN_BREADTH ** -0.5, 0.09375)
    forget_expand_map = centred(splits[8], (DECAY_RANK, HIDDEN_BREADTH), (1.0 / DECAY_RANK ** 0.5), 0.35351562, ((1, 4),))
    forget_lane_anchor = draw_forget_lane_anchor(jax.random.fold_in(splits[20], 71), 0)
    present_boost = centred(splits[10], (HIDDEN_BREADTH,), 0.5, 1.5, ((0, 4),), jnp.float32)
    content_blend_share = jnp.clip(1.0 * jax.random.uniform(splits[11], (HIDDEN_BREADTH,), jnp.float32) ** block_scale(splits[11], (HIDDEN_BREADTH,), ((0, 4),), -0.2, 0.2), 0.0, 1.0)
    forget_blend_share = jnp.clip(1.0 * jax.random.uniform(splits[12], (HIDDEN_BREADTH,), jnp.float32) ** block_scale(splits[12], (HIDDEN_BREADTH,), ((0, 4),), -0.2, 0.2), 0.0, 1.0)
    lane_normal_scale = jnp.clip(1.0 + 0.1 * jax.random.normal(splits[13], (HIDDEN_BREADTH,), jnp.float32), 0.5, 1.5)
    lane_normal_shift = centred(splits[14], (HIDDEN_BREADTH,), 0.3, 1.2, ((0, 4),), jnp.float32)
    kernel_memory_saved = centred(splits[15], (REQS, SUBSPACE_SPAN, HIDDEN_BREADTH), 1.0, 6.0, ((1, 64), (2, 4)), jnp.float32)
    prior_source_saved = centred(splits[16], (REQS, SUBSPACE_SPAN, BLEND_LANES), 1.0, 6.0, ((1, 64), (2, 4)))
    lane_owner = draw_lane_owner(jax.random.fold_in(splits[20], 71), 0)
    request_spans = draw_request_spans(jax.random.fold_in(splits[20], 71), 0)
    admitted_guesses = touch_ends(jax.random.randint(splits[19], (REQS,), 0, DRAFT + 1), jax.random.fold_in(splits[19], 1), 0, DRAFT).astype(jnp.int32)
    return dict(suffix_source=suffix_source, suffix_accept=suffix_accept, suffix_address=suffix_address, guess_lane_source=guess_lane_source, guess_lane_accept=guess_lane_accept, guess_lane_address=guess_lane_address, content_map=content_map, forget_shrink_map=forget_shrink_map, forget_expand_map=forget_expand_map, forget_lane_anchor=forget_lane_anchor, present_boost=present_boost, content_blend_share=content_blend_share, forget_blend_share=forget_blend_share, lane_normal_scale=lane_normal_scale, lane_normal_shift=lane_normal_shift, kernel_memory_saved=kernel_memory_saved, prior_source_saved=prior_source_saved, lane_owner=lane_owner, request_spans=request_spans, admitted_guesses=admitted_guesses)


HIGH = lax.Precision.HIGHEST
EPS = 0.00064

def group_norm(answer_collection, lane_normal_scale, lane_normal_shift):
    center = answer_collection - lax.optimization_barrier(jnp.mean(answer_collection, axis=-1, keepdims=True))
    spread = lax.optimization_barrier(jnp.mean(center * center, axis=-1, keepdims=True))
    normed = (center / jnp.sqrt(spread + EPS)).reshape(answer_collection.shape[0], -1)
    return (normed * lane_normal_scale + lane_normal_shift).astype(jnp.bfloat16)

def token_mix(current, previous, mixing):
    present = current.astype(jnp.float32)
    return (present + (previous.astype(jnp.float32) - present) * mixing).astype(jnp.bfloat16)

def project(mixed_value, decay_mixed_input, content_map, forget_shrink_map, forget_expand_map, forget_lane_anchor):
    content_vectors = jnp.dot(mixed_value, content_map, preferred_element_type=jnp.float32).astype(jnp.bfloat16)
    decay_low_rank = jnp.tanh(jnp.dot(decay_mixed_input, forget_shrink_map, preferred_element_type=jnp.float32)).astype(jnp.bfloat16)
    forget_logscale = -jnp.exp(forget_lane_anchor + jnp.dot(decay_low_rank, forget_expand_map, preferred_element_type=jnp.float32))
    return (content_vectors, forget_logscale)

def advance_once(ongoing_memory, accept_vectors, address_vectors, content_vectors, forget_logscale, lanes_boost):
    answer_vectors = jnp.einsum('hi,hij->hj', accept_vectors, ongoing_memory, precision=HIGH)
    answer_vectors = answer_vectors + lax.optimization_barrier(jnp.sum(accept_vectors * lanes_boost * address_vectors, axis=-1, keepdims=True)) * content_vectors
    ongoing_memory = jnp.exp(forget_logscale)[:, :, None] * ongoing_memory + address_vectors[:, :, None] * content_vectors[:, None, :]
    return (ongoing_memory, answer_vectors)

def reference(suffix_source, suffix_accept, suffix_address, guess_lane_source, guess_lane_accept, guess_lane_address, content_map, forget_shrink_map, forget_expand_map, forget_lane_anchor, present_boost, content_blend_share, forget_blend_share, lane_normal_scale, lane_normal_shift, kernel_memory_saved, prior_source_saved, lane_owner, request_spans, admitted_guesses):
    opening_memory = kernel_memory_saved.reshape(REQS, SUBSPACE_SPAN, BLEND_LANES, SUBSPACE_SPAN).transpose(0, 2, 1, 3)
    start_prev = prior_source_saved.transpose(0, 2, 1).reshape(REQS, HIDDEN_BREADTH)
    lanes_boost = present_boost.reshape(BLEND_LANES, SUBSPACE_SPAN)
    slot_long = request_spans[lane_owner] > DRAFT
    long_groups = jnp.nonzero(slot_long[::REQ_DEV], size=LONGS)[0].astype(jnp.int32)

    def divide_lanes(array):
        return array.astype(jnp.float32).reshape(array.shape[0], BLEND_LANES, SUBSPACE_SPAN)

    def prepare(tokens, first):
        previous = jnp.concatenate([first[None], tokens[:-1]], axis=0)
        content_vectors, forget_logscale = project(token_mix(tokens, previous, content_blend_share), token_mix(tokens, previous, forget_blend_share), content_map, forget_shrink_map, forget_expand_map, forget_lane_anchor)
        return (divide_lanes(content_vectors), forget_logscale.reshape(-1, BLEND_LANES, SUBSPACE_SPAN))

    def run_tail(squad_index):
        query_index = lane_owner[squad_index * REQ_DEV]
        tokens = suffix_source[squad_index]
        content_vectors, forget_logscale = prepare(tokens, start_prev[query_index])
        closing_answer, answer_collection = lax.scan(lambda threaded_pair, source_vectors: advance_once(threaded_pair, source_vectors[0], source_vectors[1], source_vectors[2], source_vectors[3], lanes_boost), opening_memory[query_index], (divide_lanes(suffix_accept[squad_index]), divide_lanes(suffix_address[squad_index]), content_vectors, forget_logscale))
        return (group_norm(answer_collection, lane_normal_scale, lane_normal_shift), closing_answer, tokens[-1])
    tail_norm, tail_end, tail_last = lax.map(run_tail, long_groups)
    tail_out = jnp.zeros((GROUPS, TAIL, HIDDEN_BREADTH), jnp.bfloat16).at[long_groups].set(tail_norm)
    end_by_group = jnp.zeros((GROUPS, BLEND_LANES, SUBSPACE_SPAN, SUBSPACE_SPAN), jnp.float32).at[long_groups].set(tail_end)
    last_by_group = jnp.zeros((GROUPS, HIDDEN_BREADTH), jnp.bfloat16).at[long_groups].set(tail_last)

    def run_draft(slot):
        query_index = lane_owner[slot]
        squad_index = slot // REQ_DEV
        trailing_pair = jnp.where(slot_long[slot], end_by_group[squad_index], opening_memory[query_index])
        first = jnp.where(slot_long[slot], last_by_group[squad_index], start_prev[query_index])
        tokens = guess_lane_source[slot]
        content_vectors, forget_logscale = prepare(tokens, first)
        count = admitted_guesses[query_index]

        def advance(threaded_pair, source_vectors):
            ongoing_memory, chosen = threaded_pair
            ongoing_memory, answer_vectors = advance_once(ongoing_memory, source_vectors[0], source_vectors[1], source_vectors[2], source_vectors[3], lanes_boost)
            chosen = jnp.where(source_vectors[4] + 1 == count, ongoing_memory, chosen)
            return ((ongoing_memory, chosen), answer_vectors)
        positions = jnp.arange(DRAFT, dtype=jnp.int32)
        (final_state, chosen), answer_collection = lax.scan(advance, (trailing_pair, trailing_pair), (divide_lanes(guess_lane_accept[slot]), divide_lanes(guess_lane_address[slot]), content_vectors, forget_logscale, positions))
        edge = jnp.where(count > 0, tokens[jnp.maximum(count - 1, 0)], first)
        return (group_norm(answer_collection, lane_normal_scale, lane_normal_shift), chosen, edge)
    draft_out, chosen, edges = lax.map(run_draft, jnp.arange(REQS, dtype=jnp.int32))
    by_request = jnp.zeros_like(chosen).at[lane_owner].set(chosen)
    state_out = by_request.transpose(0, 2, 1, 3).reshape(REQS, SUBSPACE_SPAN, HIDDEN_BREADTH)
    shift_out = jnp.zeros_like(edges).at[lane_owner].set(edges).reshape(REQS, BLEND_LANES, SUBSPACE_SPAN).transpose(0, 2, 1)
    return (tail_out, draft_out, state_out, shift_out)
```

```python
import jax
import jax.numpy as jnp
from jax import lax
from jax.experimental import pallas as pl
from jax.experimental.pallas import tpu as pltpu
from jax.sharding import PartitionSpec as P

SPAN = 64
DRAFT = 16
EPS = 0.00064
REP = 64
TP = 4
WID = 1024
TAIL = 384
HALF = 192
LATE = 48
ROWS = HALF + LATE
PIECE = 48
CHUNK = 32
PAIRS = 8
RANK = 128
F32 = jnp.float32
BF16 = jnp.bfloat16
MESH = pl.DeviceIdType.MESH

ITEMS = (
    ("x", 0, 48),
    ("x", 48, 48),
    ("x", 96, 48),
    ("x", 144, 48),
    ("p", 0, 192),
    ("x", 192, 16),
    ("x", 208, 32),
    ("p", 192, 48),
)
RELAY_RIGHT = (0, 2, 4, 5, 7)


def iota(shape, dim):
    return lax.broadcasted_iota(jnp.int32, shape, dim)


def nt(a, b):
    return lax.dot_general(a, b, (((1,), (1,)), ((), ())), preferred_element_type=F32)


def tn(a, b):
    return lax.dot_general(a, b, (((0,), (0,)), ((), ())), preferred_element_type=F32)


def mm(a, b):
    return jnp.dot(a, b, preferred_element_type=F32)


def owner_tables(own_ref, spans_ref, adm_ref, perm_ref):
    hot = (iota((128, 128), 0) == own_ref[...]).astype(F32)
    row = iota((8, 128), 0)
    long_q = (spans_ref[...] > DRAFT).astype(F32)
    facts = jnp.where(row == 0, long_q, jnp.where(row == 1, adm_ref[...].astype(F32), 0.0))
    by_slot = mm(facts.astype(BF16), hot.astype(BF16))
    perm_ref[...] = hot.T
    dealt = jnp.concatenate([perm_ref[pl.ds(0, 64, stride=2), :], perm_ref[pl.ds(1, 64, stride=2), :]], axis=0)
    return dealt, by_slot


def fact(by_slot, row, slot):
    pick = iota((8, 128), 1) == slot
    here = jnp.where(pick & (iota((8, 128), 0) == row), by_slot, 0.0)
    return jnp.sum(jnp.sum(here, axis=1, keepdims=True), axis=0, keepdims=True)


def greet_rep(barrier, g, t):
    def one(d, _):
        pl.semaphore_signal(barrier, inc=1, device_id=(lax.rem(g + d, REP), t), device_id_type=MESH)
        return 0

    lax.fori_loop(1, REP, one, 0)


def scatter_rep(src, dst, send, recv, g, t):
    def one(d, _):
        to = lax.rem(g + d, REP)
        pltpu.make_async_remote_copy(
            src_ref=src.at[to],
            dst_ref=dst.at[g],
            send_sem=send,
            recv_sem=recv,
            device_id=(to, t),
            device_id_type=MESH,
        ).start()
        return 0

    lax.fori_loop(1, REP, one, 0)


def wait_rep(buf, sem):
    part = buf.at[pl.ds(0, REP - 1)]
    pltpu.make_async_copy(part, part, sem).wait()


def mixed(x, prev, share):
    return x + (prev - x) * share


def gather_kernel(
    x_ref, gx_ref, km_ref, p0_ref, mc_ref, mf_ref, own_ref, spans_ref, adm_ref, w_hbm, sh_hbm,
    got_ref, vt_ref, lt_ref, vl_ref, ll_ref, first_ref,
    w_ref, sh_ref, perm_ref, wide_ref, sbuf, pbuf, pgot, xv_ref, part_ref, xin, pin, xg, pg, acc, vh, lh,
    w_sem, sh_sem, st_send, st_recv, p_send, p_recv, pair_send, pair_recv,
    right_send, left_recv, left_send, right_recv, hop_send, hop_recv, back_send, back_recv,
):
    g, t = lax.axis_index("rep"), lax.axis_index("tp")
    core = lax.rem(g, 2)
    mate = g + 1 - 2 * core
    right, left, far = lax.rem(t + 1, TP), lax.rem(t + 3, TP), lax.rem(t + 2, TP)
    mine = pl.multiple_of(core * HALF, 16)
    other = pl.multiple_of((1 - core) * HALF, 16)

    def w_copy(k):
        rows = pl.ds(k * WID, WID)
        return pltpu.make_async_copy(w_hbm.at[rows], w_ref.at[rows], w_sem.at[k])

    sh_copy = pltpu.make_async_copy(sh_hbm.at[pl.ds(pl.multiple_of(t * WID, WID), WID)], sh_ref, sh_sem)
    sh_copy.start()
    for k in range(TP):
        w_copy(k).start()

    barrier = pltpu.get_barrier_semaphore()
    greet_rep(barrier, g, t)
    for d in range(1, TP):
        pl.semaphore_signal(barrier, inc=1, device_id=(g, lax.rem(t + d, TP)), device_id_type=MESH)

    dealt, by_slot = owner_tables(own_ref, spans_ref, adm_ref, perm_ref)
    dealt = dealt.astype(BF16)
    long_own = fact(by_slot, 0, 2 * g) > 0.5

    sent = nt(dealt, p0_ref[...])
    wide_ref[...] = jnp.zeros_like(wide_ref)
    wide_ref[pl.ds(0, 64, stride=8), 0:16] = sent[0:64]
    wide_ref[pl.ds(1, 64, stride=8), 0:16] = sent[64:128]
    pbuf[...] = wide_ref[0:512, :].astype(BF16).reshape(64, 8, 128)
    pgot[g] = pbuf[g]
    for c in range(8):
        rows = mm(dealt, km_ref[pl.ds(c, 128, stride=8), :].astype(BF16))
        wide_ref[pl.ds(c, 64, stride=16), :] = rows[0:64]
        wide_ref[pl.ds(8 + c, 64, stride=16), :] = rows[64:128]
    sbuf[...] = wide_ref[...].astype(BF16).reshape(64, 16, 128)
    got_ref[g] = sbuf[g]

    mc, mf = mc_ref[...], mf_ref[...]
    sh_copy.wait()

    def mix_rows(j, _):
        r0 = pl.multiple_of(j * PIECE, 16)
        x = x_ref[pl.ds(r0, PIECE), :].astype(F32)
        ahead = x_ref[pl.ds(pl.multiple_of(jnp.maximum(r0 - 16, 0), 16), 16), :].astype(F32)
        prev = jnp.where(iota((PIECE, WID), 0) == 0, ahead[15:16], pltpu.roll(x, 1, 0))
        xv_ref[pl.ds(r0, PIECE), :] = mixed(x, prev, mc).astype(BF16)
        part_ref[pl.ds(r0, PIECE), :] = mm(mixed(x, prev, mf).astype(BF16), sh_ref[...]).astype(BF16)
        return 0

    lax.fori_loop(0, TAIL // PIECE, mix_rows, 0)

    pl.semaphore_wait(barrier, REP - 1 + TP - 1)

    def pair_copy(j):
        if j < 4:
            src, dst = xv_ref.at[pl.ds(other + j * PIECE, PIECE)], xin.at[pl.ds(j * PIECE, PIECE)]
        else:
            src, dst = part_ref.at[pl.ds(other, HALF)], pin
        return pltpu.make_async_remote_copy(
            src_ref=src,
            dst_ref=dst,
            send_sem=pair_send.at[j],
            recv_sem=pair_recv.at[j],
            device_id=(mate, t),
            device_id_type=MESH,
        )

    def part_of(item, source):
        kind, r0, n = ITEMS[item]
        return (xg if kind == "x" else pg).at[source, pl.ds(r0, n)]

    def move(item, source, to, send, recv):
        return pltpu.make_async_remote_copy(
            src_ref=part_of(item, source),
            dst_ref=part_of(item, source),
            send_sem=send.at[item],
            recv_sem=recv.at[item],
            device_id=(g, to),
            device_id_type=MESH,
        )

    def give(item):
        move(item, t, right, right_send, left_recv).start()
        move(item, t, left, left_send, right_recv).start()

    for j in range(5):
        pair_copy(j).start()
    scatter_rep(pbuf, pgot, p_send, p_recv, g, t)
    for j in range(4):
        pair_copy(j).wait_recv()
        rows = pl.ds(j * PIECE, PIECE)
        xg[t, rows, :] = jnp.where(long_own, xv_ref[pl.ds(mine + j * PIECE, PIECE), :], xin[rows, :])
        give(j)
    pair_copy(4).wait_recv()
    pg[t, 0:HALF, :] = jnp.where(long_own, part_ref[pl.ds(mine, HALF), :], pin[...])
    give(4)
    scatter_rep(sbuf, got_ref, st_send, st_recv, g, t)

    wait_rep(pgot, p_recv)
    wide_ref[0:512, :] = pgot[...].reshape(512, 128).astype(F32)
    spread = (iota((128, WID), 1) // SPAN == iota((128, WID), 0)).astype(BF16)
    own_lane = iota((64, WID), 1) % SPAN == iota((64, WID), 0)
    before = []
    for s in range(2):
        vals = mm(wide_ref[pl.ds(s, 64, stride=8), :].astype(BF16), spread)
        before.append(jnp.sum(jnp.where(own_lane, vals, 0.0), axis=0, keepdims=True))
    final = x_ref[TAIL - 16 : TAIL, :].astype(F32)[15:16]
    firsts = [jnp.where(long_own, final, before[0]), before[1]]
    row8 = iota((8, WID), 0)
    first_ref[...] = jnp.where(row8 == 0, firsts[0], firsts[1])
    head = x_ref[0:16, :].astype(F32)
    cur = [gx_ref[0:16, :].astype(F32), gx_ref[16:32, :].astype(F32), head]
    row16 = iota((16, WID), 0)
    ahead = [jnp.where(row16 == 0, f, pltpu.roll(x, 1, 0)) for x, f in zip(cur, firsts + before[:1])]
    for s in range(3):
        xg[t, HALF + 16 * s : HALF + 16 * s + 16, :] = mixed(cur[s], ahead[s], mc).astype(BF16)
        pg[t, HALF + 16 * s : HALF + 16 * s + 16, :] = mm(
            mixed(cur[s], ahead[s], mf).astype(BF16), sh_ref[...]
        ).astype(BF16)
    for item in range(5, 8):
        give(item)

    def product(source, add):
        def tile(n, _):
            cols = pl.ds(pl.multiple_of(n * 256, 256), 256)
            out = mm(xg[source], w_ref[pl.ds(pl.multiple_of(source * WID, WID), WID), cols])
            acc[:, cols] = acc[:, cols] + out if add else out
            return 0

        lax.fori_loop(0, WID // 256, tile, 0)

    for k in range(TP):
        w_copy(k).wait()
    product(t, False)
    for item in range(8):
        move(item, left, right, right_send, left_recv).wait_recv()
        if item in RELAY_RIGHT:
            move(item, left, right, hop_send, hop_recv).start()
        move(item, right, left, left_send, right_recv).wait_recv()
        if item not in RELAY_RIGHT:
            move(item, right, left, hop_send, hop_recv).start()
    product(left, True)
    product(right, True)
    for item in range(8):
        move(item, far, right, hop_send, hop_recv).wait_recv()
    low = jnp.tanh(pg[0].astype(F32) + pg[1].astype(F32) + pg[2].astype(F32) + pg[3].astype(F32)).astype(BF16)
    lh[...] = low[0:HALF]
    ll_ref[...] = low[HALF:ROWS]
    lt_ref[pl.ds(mine, HALF), :] = low[0:HALF]
    product(far, True)
    vh[...] = acc[0:HALF, :].astype(BF16)

    def back_copy(src, dst, k):
        return pltpu.make_async_remote_copy(
            src_ref=src,
            dst_ref=dst.at[pl.ds(mine, HALF)],
            send_sem=back_send.at[k],
            recv_sem=back_recv.at[k],
            device_id=(mate, t),
            device_id_type=MESH,
        )

    backs = [back_copy(lh, lt_ref, 0), back_copy(vh, vt_ref, 1)]
    for b in backs:
        b.start()
    vt_ref[pl.ds(mine, HALF), :] = vh[...]
    vl_ref[...] = acc[HALF:ROWS, :].astype(BF16)
    wait_rep(got_ref, st_recv)
    wait_rep(pbuf, p_send)
    wait_rep(sbuf, st_send)
    for j in range(5):
        pair_copy(j).wait_send()
    for item in range(8):
        move(item, t, right, right_send, left_recv).wait_send()
        move(item, t, left, left_send, right_recv).wait_send()
        move(item, far, right, hop_send, hop_recv).wait_send()
    for b in backs:
        b.wait()
    vt_ref[0:16, :] = jnp.where(row16 == 0, vl_ref[32:33, :], vt_ref[0:16, :])
    lt_ref[0:16, :] = jnp.where(iota((16, RANK), 0) == 0, ll_ref[32:33, :], lt_ref[0:16, :])


def halves(a):
    low = iota(a.shape, 1) < SPAN
    zero = jnp.zeros_like(a)
    return jnp.concatenate([jnp.where(low, a, zero), jnp.where(low, zero, a)], axis=0)


def lanes(p):
    return slice(128 * p, 128 * p + 128)


def running(log, n):
    tri = (iota((n, n), 0) >= iota((n, n), 1)).astype(BF16)
    hi = log.astype(BF16)
    lo = (log - hi.astype(F32)).astype(BF16)
    return mm(tri, hi) + mm(tri, lo)


def answers(r, k, v, incl, log, boost, states, heads_sum, n):
    excl = incl - log
    mid = incl[n // 2 : n // 2 + 1]
    q = (r * jnp.exp(jnp.minimum(excl - mid, 80.0))).astype(BF16)
    kk = (k * jnp.exp(jnp.minimum(mid - incl, 80.0))).astype(BF16)
    ri = (r * jnp.exp(excl)).astype(BF16)
    own = (r * boost * k).astype(BF16)
    gain = mm(jnp.concatenate([own[:, lanes(p)] for p in range(PAIRS)], axis=0), heads_sum)
    strict = iota((2 * n, n), 0) % n > iota((2 * n, n), 1)
    low = iota((n, 128), 1) < SPAN
    out = []
    for p in range(PAIRS):
        c = lanes(p)
        score = jnp.where(strict, nt(halves(q[:, c]), kk[:, c]), 0.0).astype(BF16)
        both = mm(score, v[:, c])
        y = jnp.where(low, both[0:n], both[n : 2 * n])
        y = y + nt(ri[:, c], states[p].astype(BF16))
        out.append(y + gain[n * p : n * p + n] * v[:, c].astype(F32))
    return jnp.concatenate(out, axis=0)


def normed(y, heads_sum, scale, shift, n):
    hi = y.astype(BF16)
    lo = (y - hi.astype(F32)).astype(BF16)
    center = y - (mm(hi, heads_sum) + mm(lo, heads_sum)) * (1.0 / SPAN)
    spread = mm((center * center).astype(BF16), heads_sum) * (1.0 / SPAN)
    o = center * lax.rsqrt(spread + EPS)
    return jnp.concatenate(
        [o[n * p : n * p + n] * scale[:, lanes(p)] + shift[:, lanes(p)] for p in range(PAIRS)], axis=1
    )


def mix_kernel(
    rt_ref, kt_ref, gx_ref, gr_ref, gk_ref, vt_ref, lt_ref, vl_ref, ll_ref, got_ref, first_ref,
    ex_ref, anchor_ref, boost_ref, scale_ref, shift_ref, own_ref, spans_ref, adm_ref,
    tail_ref, draft_ref, state_ref, prior_ref,
    perm_ref, wide_ref, st_ref, sbuf, sgot, ebuf, egot, s_send, s_recv, e_send, e_recv,
):
    g, t = lax.axis_index("rep"), lax.axis_index("tp")
    barrier = pltpu.get_barrier_semaphore()
    greet_rep(barrier, g, t)
    dealt, by_slot = owner_tables(own_ref, spans_ref, adm_ref, perm_ref)
    long_own = fact(by_slot, 0, 2 * g) > 0.5
    boost, scale, shift = boost_ref[...], scale_ref[...], shift_ref[...]
    anchor = anchor_ref[...]
    same = iota((128, 128), 0) // SPAN == iota((128, 128), 1) // SPAN
    heads_sum = same.astype(BF16)

    spread = (iota((128, WID), 1) // SPAN == iota((128, WID), 0)).astype(BF16)
    own_lane = iota((64, WID), 1) % SPAN == iota((64, WID), 0)
    row16 = iota((DRAFT, WID), 0)
    counts = []
    wide_ref[0:512, :] = jnp.zeros((512, 128), F32)
    for s in range(2):
        count = fact(by_slot, 1, 2 * g + s).astype(jnp.int32)
        counts.append(count)
        rows = gx_ref[DRAFT * s : DRAFT * s + DRAFT, :].astype(F32)
        edge = jnp.sum(jnp.where(row16 == count - 1, rows, 0.0), axis=0, keepdims=True)
        edge = jnp.where(count > 0, edge, first_ref[s : s + 1, :])
        wide_ref[pl.ds(s, 64, stride=8), :] = nt(jnp.where(own_lane, edge, 0.0).astype(BF16), spread)
    ebuf[...] = wide_ref[0:512, :].astype(BF16).reshape(64, 8, 128)
    egot[g] = ebuf[g]

    wide_ref[...] = got_ref[...].reshape(1024, 128).astype(F32)
    for s in range(2):
        for p in range(PAIRS):
            rows = wide_ref[pl.ds(8 * s + p, 64, stride=16), :]
            st_ref[s, p] = halves(rows).T

    pl.semaphore_wait(barrier, REP - 1)
    scatter_rep(ebuf, egot, e_send, e_recv, g, t)

    st0 = [st_ref[0, p] for p in range(PAIRS)]

    def chunk(i, _):
        rows = pl.ds(pl.multiple_of(i * CHUNK, 16), CHUNK)
        log = -jnp.exp(anchor + mm(lt_ref[rows, :], ex_ref[...]))
        r, k, v = rt_ref[rows, :].astype(F32), kt_ref[rows, :].astype(F32), vt_ref[rows, :]
        incl = running(log, CHUNK)
        states = [st_ref[2, p] for p in range(PAIRS)]
        y = answers(r, k, v, incl, log, boost, states, heads_sum, CHUNK)
        last = incl[CHUNK - 1 : CHUNK]
        kd = (k * jnp.exp(last - incl)).astype(BF16)
        keep = jnp.exp(last)
        for p in range(PAIRS):
            c = lanes(p)
            st_ref[2, p] = states[p] * keep[:, c] + jnp.where(same, tn(v[:, c], kd[:, c]), 0.0)
        o = normed(y, heads_sum, scale, shift, CHUNK)
        tail_ref[rows, :] = jnp.where(long_own, o, 0.0).astype(BF16)
        return 0

    for p in range(PAIRS):
        st_ref[2, p] = st_ref[0, p]
    lax.fori_loop(0, TAIL // CHUNK, chunk, 0)

    for s in range(2):
        rows = slice(DRAFT * s, DRAFT * s + DRAFT)
        log = -jnp.exp(anchor + mm(ll_ref[rows, :], ex_ref[...]))
        r, k, v = gr_ref[rows, :].astype(F32), gk_ref[rows, :].astype(F32), vl_ref[rows, :]
        incl = running(log, DRAFT)
        if s == 0:
            states = [jnp.where(long_own, st_ref[2, p], st_ref[0, p]) for p in range(PAIRS)]
        else:
            states = [st_ref[1, p] for p in range(PAIRS)]
        y = answers(r, k, v, incl, log, boost, states, heads_sum, DRAFT)
        draft_ref[rows, :] = normed(y, heads_sum, scale, shift, DRAFT).astype(BF16)
        taken = row16 < counts[s]
        upto = jnp.sum(jnp.where(taken, log, 0.0), axis=0, keepdims=True)
        weight = jnp.where(taken, jnp.exp(jnp.where(taken, upto - incl, 0.0)), 0.0)
        kd = (k * weight).astype(BF16)
        keep = jnp.exp(upto)
        for p in range(PAIRS):
            c = lanes(p)
            end = (states[p] * keep[:, c] + jnp.where(same, tn(v[:, c], kd[:, c]), 0.0)).T
            wide_ref[pl.ds(8 * s + p, 64, stride=16), :] = end[0:64] + end[64:128]
    sbuf[...] = wide_ref[...].astype(BF16).reshape(64, 16, 128)
    sgot[g] = sbuf[g]
    scatter_rep(sbuf, sgot, s_send, s_recv, g, t)

    hot = dealt.astype(BF16)
    wait_rep(egot, e_recv)
    wide_ref[0:512, :] = egot[...].reshape(512, 128).astype(F32)
    edges = jnp.concatenate([wide_ref[pl.ds(0, 64, stride=8), :], wide_ref[pl.ds(1, 64, stride=8), :]], axis=0)
    prior_ref[...] = tn(edges.astype(BF16), hot)[0:16].astype(BF16)
    by_req = dealt.T.astype(BF16)
    wait_rep(sgot, s_recv)
    wide_ref[...] = sgot[...].reshape(1024, 128).astype(F32)
    for c in range(8):
        rows = jnp.concatenate(
            [wide_ref[pl.ds(c, 64, stride=16), :], wide_ref[pl.ds(8 + c, 64, stride=16), :]], axis=0
        )
        state_ref[pl.ds(c, 128, stride=8), :] = mm(by_req, rows.astype(BF16))
    wait_rep(ebuf, e_send)
    wait_rep(sbuf, s_send)


VM = pl.BlockSpec(memory_space=pltpu.VMEM)
ANY = pl.BlockSpec(memory_space=pl.ANY)
DMA = pltpu.SemaphoreType.DMA


def local(
    suffix_source, suffix_accept, suffix_address, guess_lane_source, guess_lane_accept, guess_lane_address,
    content_map, forget_shrink_map, forget_expand_map, forget_lane_anchor, present_boost,
    content_blend_share, forget_blend_share, lane_normal_scale, lane_normal_shift,
    kernel_memory_saved, prior_source_saved, lane_owner, request_spans, admitted_guesses,
):
    gx = guess_lane_source.reshape(2 * DRAFT, WID)
    small = [a.reshape(1, 128) for a in (lane_owner, request_spans, admitted_guesses)]
    sds = jax.ShapeDtypeStruct
    got, vt, lt, vl, ll, first = pl.pallas_call(
        gather_kernel,
        name="gather_project",
        out_shape=(
            sds((REP, 16, 128), BF16),
            sds((TAIL, WID), BF16),
            sds((TAIL, RANK), BF16),
            sds((LATE, WID), BF16),
            sds((LATE, RANK), BF16),
            sds((8, WID), F32),
        ),
        in_specs=[VM] * 9 + [ANY, ANY],
        out_specs=(VM,) * 6,
        scratch_shapes=[
            pltpu.VMEM((TP * WID, WID), BF16),
            pltpu.VMEM((WID, RANK), BF16),
            pltpu.VMEM((128, 128), F32),
            pltpu.VMEM((1024, 128), F32),
            pltpu.VMEM((REP, 16, 128), BF16),
            pltpu.VMEM((REP, 8, 128), BF16),
            pltpu.VMEM((REP, 8, 128), BF16),
            pltpu.VMEM((TAIL, WID), BF16),
            pltpu.VMEM((TAIL, RANK), BF16),
            pltpu.VMEM((HALF, WID), BF16),
            pltpu.VMEM((HALF, RANK), BF16),
            pltpu.VMEM((TP, ROWS, WID), BF16),
            pltpu.VMEM((TP, ROWS, RANK), BF16),
            pltpu.VMEM((ROWS, WID), F32),
            pltpu.VMEM((HALF, WID), BF16),
            pltpu.VMEM((HALF, RANK), BF16),
            DMA((TP,)), DMA, DMA, DMA, DMA, DMA, DMA((5,)), DMA((5,)),
            DMA((8,)), DMA((8,)), DMA((8,)), DMA((8,)), DMA((8,)), DMA((8,)), DMA((2,)), DMA((2,)),
        ],
        compiler_params=pltpu.CompilerParams(
            collective_id=0, has_side_effects=True, vmem_limit_bytes=48 << 20
        ),
    )(
        suffix_source.reshape(TAIL, WID),
        gx,
        kernel_memory_saved.reshape(1024, 128),
        prior_source_saved.reshape(128, 16).T,
        content_blend_share.reshape(1, WID),
        forget_blend_share.reshape(1, WID),
        *small,
        content_map,
        forget_shrink_map,
    )
    tail, draft, state, prior = pl.pallas_call(
        mix_kernel,
        name="mix_return",
        out_shape=(
            sds((TAIL, WID), BF16),
            sds((2 * DRAFT, WID), BF16),
            sds((1024, 128), F32),
            sds((16, 128), BF16),
        ),
        in_specs=[VM] * 19,
        out_specs=(VM,) * 4,
        scratch_shapes=[
            pltpu.VMEM((128, 128), F32),
            pltpu.VMEM((1024, 128), F32),
            pltpu.VMEM((3, PAIRS, 128, 128), F32),
            pltpu.VMEM((REP, 16, 128), BF16),
            pltpu.VMEM((REP, 16, 128), BF16),
            pltpu.VMEM((REP, 8, 128), BF16),
            pltpu.VMEM((REP, 8, 128), BF16),
            DMA, DMA, DMA, DMA,
        ],
        compiler_params=pltpu.CompilerParams(
            collective_id=1, has_side_effects=True, vmem_limit_bytes=48 << 20
        ),
    )(
        suffix_accept.reshape(TAIL, WID),
        suffix_address.reshape(TAIL, WID),
        gx,
        guess_lane_accept.reshape(2 * DRAFT, WID),
        guess_lane_address.reshape(2 * DRAFT, WID),
        vt, lt, vl, ll, got, first,
        forget_expand_map,
        forget_lane_anchor.reshape(1, WID),
        present_boost.reshape(1, WID),
        lane_normal_scale.reshape(1, WID),
        lane_normal_shift.reshape(1, WID),
        *small,
    )
    return (
        tail.reshape(1, TAIL, WID),
        draft.reshape(2, DRAFT, WID),
        state.reshape(128, 1, WID),
        prior.T.reshape(128, 1, 16),
    )


def solution(mesh):
    rows, cols, chan = P("rep", None, "tp"), P(None, "tp"), P("tp")
    cache = P(None, "rep", "tp")
    return jax.shard_map(
        local,
        mesh=mesh,
        in_specs=(rows,) * 6 + (cols, P(), cols) + (chan,) * 6 + (cache, cache, P(), P(), P()),
        out_specs=(rows, rows, cache, cache),
        check_vma=False,
    )
```

```python
import jax
import jax.numpy as jnp
from jax import lax
from jax.experimental import pallas as pl
from jax.experimental.pallas import tpu as pltpu
from jax.sharding import PartitionSpec as P

SPAN = 64
DRAFT = 16
EPS = 0.00064
REP = 64
TP = 4
WID = 1024
TAIL = 384
HALF = 192
LATE = 48
ROWS = HALF + LATE
PIECE = 48
CHUNK = 32
PAIRS = 8
RANK = 128
F32 = jnp.float32
BF16 = jnp.bfloat16
MESH = pl.DeviceIdType.MESH

SIDE = WID // 2
SPLIT = PAIRS // 2
STEPS = TAIL // CHUNK

ITEMS = (
    ("p", 0, 192),
    ("x", 0, 48),
    ("x", 48, 48),
    ("x", 96, 48),
    ("x", 144, 48),
    ("x", 192, 16),
    ("x", 208, 32),
    ("p", 192, 48),
)
RELAY_RIGHT = (0, 1, 3, 5, 7)


def iota(shape, dim):
    return lax.broadcasted_iota(jnp.int32, shape, dim)


def nt(a, b):
    return lax.dot_general(a, b, (((1,), (1,)), ((), ())), preferred_element_type=F32)


def tn(a, b):
    return lax.dot_general(a, b, (((0,), (0,)), ((), ())), preferred_element_type=F32)


def mm(a, b):
    return jnp.dot(a, b, preferred_element_type=F32)


def owner_tables(own_ref, spans_ref, adm_ref, perm_ref):
    hot = (iota((128, 128), 0) == own_ref[...]).astype(F32)
    row = iota((8, 128), 0)
    long_q = (spans_ref[...] > DRAFT).astype(F32)
    facts = jnp.where(row == 0, long_q, jnp.where(row == 1, adm_ref[...].astype(F32), 0.0))
    by_slot = mm(facts.astype(BF16), hot.astype(BF16))
    perm_ref[...] = hot.T
    dealt = jnp.concatenate([perm_ref[pl.ds(0, 64, stride=2), :], perm_ref[pl.ds(1, 64, stride=2), :]], axis=0)
    return dealt, by_slot


def fact(by_slot, row, slot):
    pick = iota((8, 128), 1) == slot
    here = jnp.where(pick & (iota((8, 128), 0) == row), by_slot, 0.0)
    return jnp.sum(jnp.sum(here, axis=1, keepdims=True), axis=0, keepdims=True)


def greet_rep(barrier, g, t):
    def one(d, _):
        pl.semaphore_signal(barrier, inc=1, device_id=(lax.rem(g + d, REP), t), device_id_type=MESH)
        return 0

    lax.fori_loop(1, REP, one, 0)


def scatter_rep(src, dst, send, recv, g, t):
    def one(d, _):
        to = lax.rem(g + d, REP)
        pltpu.make_async_remote_copy(
            src_ref=src.at[to],
            dst_ref=dst.at[g],
            send_sem=send,
            recv_sem=recv,
            device_id=(to, t),
            device_id_type=MESH,
        ).start()
        return 0

    lax.fori_loop(1, REP, one, 0)


def wait_rep(buf, sem):
    part = buf.at[pl.ds(0, REP - 1)]
    pltpu.make_async_copy(part, part, sem).wait()


def mixed(x, prev, share):
    return x + (prev - x) * share


def halves(a):
    low = iota(a.shape, 1) < SPAN
    zero = jnp.zeros_like(a)
    return jnp.concatenate([jnp.where(low, a, zero), jnp.where(low, zero, a)], axis=0)


def lanes(p):
    return slice(128 * p, 128 * p + 128)


def stack(a, pairs):
    return jnp.concatenate([a[:, lanes(p)] for p in range(pairs)], axis=0)


def running(log, n):
    tri = (iota((n, n), 0) >= iota((n, n), 1)).astype(BF16)
    hi = log.astype(BF16)
    lo = (log - hi.astype(F32)).astype(BF16)
    return mm(tri, hi) + mm(tri, lo)


def column(row):
    hi = row.astype(BF16).astype(F32)
    rest = row - hi
    mid = rest.astype(BF16).astype(F32)
    low = rest - mid
    at = iota((16, 128), 0)
    parts = jnp.where(at == 0, hi, jnp.where(at == 1, mid, jnp.where(at == 2, low, 0.0)))
    return tn(parts.astype(BF16), jnp.ones((16, 128), BF16))


def scaled(r, k, incl, log, n):
    excl = incl - log
    mid = incl[n // 2 : n // 2 + 1]
    q = (r * jnp.exp(jnp.minimum(excl - mid, 80.0))).astype(BF16)
    kk = (k * jnp.exp(jnp.minimum(mid - incl, 80.0))).astype(BF16)
    return q, kk, (r * jnp.exp(excl)).astype(BF16)


def scored(q, kk, n):
    strict = iota((2 * n, n), 0) % n > iota((2 * n, n), 1)
    return jnp.where(strict, nt(halves(q), kk), 0.0).astype(BF16)


def normed(y, heads_sum, scale, shift, n, pairs):
    hi = y.astype(BF16)
    lo = (y - hi.astype(F32)).astype(BF16)
    center = y - (mm(hi, heads_sum) + mm(lo, heads_sum)) * (1.0 / SPAN)
    spread = mm((center * center).astype(BF16), heads_sum) * (1.0 / SPAN)
    o = center * lax.rsqrt(spread + EPS)
    return jnp.concatenate(
        [o[n * p : n * p + n] * scale[:, lanes(p)] + shift[:, lanes(p)] for p in range(pairs)], axis=1
    )


def mix_kernel(
    x_hbm, gx_hbm, km_hbm, p0_hbm, mc_hbm, mf_hbm, own_hbm, spans_hbm, adm_hbm, gr_hbm, gk_hbm, ex_hbm,
    anchor_hbm, boost_hbm, scale_hbm, shift_hbm, w_hbm, sh_hbm, rt_hbm, kt_hbm,
    tail_ref, draft_ref, state_ref, prior_ref,
    x_ref, gx_ref, km_ref, p0_ref, mc_ref, mf_ref, own_ref, spans_ref, adm_ref, gr_ref, gk_ref, ex_ref,
    anchor_ref, boost_ref, scale_ref, shift_ref, w_ref, sh_ref, rown, kown,
    perm_ref, wide_ref, sbuf, sgot, pbuf, pgot, xv_ref, part_ref, xin, pin, zsend, zpart, zin, zpin,
    xg, pg, acc, vh, lh, vl_ref, ll_ref, first_ref, vt_ref, lt_ref, rmate, kmate, st0_ref, stm_ref,
    sc_ref, ri_ref, gain_ref, kd_ref, keep_ref, st_ref, endm_ref, y_ref, o_ref, om_ref,
    dy_ref, dri_ref, du_ref, dk_ref, rbuf, rgot, ebuf, egot,
    in_sem, w_sem, st_send, st_recv, p_send, p_recv, e_send, e_recv, b_send, b_recv, mate_send, mate_recv,
    right_send, left_recv, left_send, right_recv, hop_send, hop_recv,
):
    g, t = lax.axis_index("rep"), lax.axis_index("tp")
    core = lax.rem(g, 2)
    mate = g + 1 - 2 * core
    right, left, far = lax.rem(t + 1, TP), lax.rem(t + 3, TP), lax.rem(t + 2, TP)
    mine = pl.multiple_of(core * HALF, 16)
    other = pl.multiple_of((1 - core) * HALF, 16)
    cols = pl.ds(pl.multiple_of(core * SIDE, 128), SIDE)
    mate_cols = pl.ds(pl.multiple_of((1 - core) * SIDE, 128), SIDE)

    own_rows = pl.ds(pl.multiple_of(t * WID, WID), WID)
    plain = (
        (x_hbm, x_ref), (mf_hbm, mf_ref), (mc_hbm, mc_ref), (sh_hbm.at[own_rows], sh_ref), (own_hbm, own_ref),
        (spans_hbm, spans_ref), (adm_hbm, adm_ref), (p0_hbm, p0_ref), (gx_hbm, gx_ref), (km_hbm, km_ref),
        (rt_hbm.at[:, cols], rown), (kt_hbm.at[:, cols], kown), (gr_hbm, gr_ref), (gk_hbm, gk_ref), (ex_hbm, ex_ref),
        (anchor_hbm, anchor_ref), (boost_hbm, boost_ref), (scale_hbm, scale_ref), (shift_hbm, shift_ref),
    )

    def in_copy(i):
        return pltpu.make_async_copy(plain[i][0], plain[i][1], in_sem.at[i])

    def w_copy(k):
        rows = pl.ds(k * WID, WID)
        return pltpu.make_async_copy(w_hbm.at[rows], w_ref.at[rows], w_sem.at[k])

    for i in range(len(plain)):
        in_copy(i).start()
    for k in range(TP):
        w_copy(k).start()

    barrier = pltpu.get_barrier_semaphore()
    greet_rep(barrier, g, t)
    for d in range(1, TP):
        pl.semaphore_signal(barrier, inc=1, device_id=(g, lax.rem(t + d, TP)), device_id_type=MESH)

    for i in range(4):
        in_copy(i).wait()
    mc, mf = mc_ref[...], mf_ref[...]

    def mix_rows(j, _):
        r0 = pl.multiple_of(j * PIECE, 16)
        x = x_ref[pl.ds(r0, PIECE), :].astype(F32)
        ahead = x_ref[pl.ds(pl.multiple_of(jnp.maximum(r0 - 16, 0), 16), 16), :].astype(F32)
        prev = jnp.where(iota((PIECE, WID), 0) == 0, ahead[15:16], pltpu.roll(x, 1, 0))
        xv_ref[pl.ds(r0, PIECE), :] = mixed(x, prev, mc).astype(BF16)
        part_ref[pl.ds(r0, PIECE), :] = mm(mixed(x, prev, mf).astype(BF16), sh_ref[...]).astype(BF16)
        return 0

    lax.fori_loop(0, TAIL // PIECE, mix_rows, 0)
    for i in range(4, len(plain)):
        in_copy(i).wait()
    pl.semaphore_wait(barrier, REP - 1 + TP - 1)

    moves = {
        0: (part_ref.at[pl.ds(other, HALF)], pin),
        5: (rt_hbm.at[:, mate_cols], rmate),
        6: (kt_hbm.at[:, mate_cols], kmate),
        7: (zsend, zin),
        8: (zpart, zpin),
        9: (lh, lt_ref.at[pl.ds(mine, HALF)]),
        10: (vh.at[:, mate_cols], vt_ref.at[pl.ds(mine, HALF)]),
        11: (st0_ref.at[pl.ds((1 - core) * SPLIT, SPLIT)], stm_ref),
        12: (st_ref, endm_ref),
        13: (o_ref, om_ref),
    }
    for j in range(4):
        moves[1 + j] = (xv_ref.at[pl.ds(other + j * PIECE, PIECE)], xin.at[pl.ds(j * PIECE, PIECE)])

    def to_mate(j):
        return pltpu.make_async_remote_copy(
            src_ref=moves[j][0],
            dst_ref=moves[j][1],
            send_sem=mate_send.at[j],
            recv_sem=mate_recv.at[j],
            device_id=(mate, t),
            device_id_type=MESH,
        )

    def part_of(item, source):
        kind, r0, n = ITEMS[item]
        return (xg if kind == "x" else pg).at[source, pl.ds(r0, n)]

    def move(item, source, to, send, recv):
        return pltpu.make_async_remote_copy(
            src_ref=part_of(item, source),
            dst_ref=part_of(item, source),
            send_sem=send.at[item],
            recv_sem=recv.at[item],
            device_id=(g, to),
            device_id_type=MESH,
        )

    def give(item):
        move(item, t, right, right_send, left_recv).start()
        move(item, t, left, left_send, right_recv).start()

    def hand_on(item):
        move(item, left, right, right_send, left_recv).wait_recv()
        if item in RELAY_RIGHT:
            move(item, left, right, hop_send, hop_recv).start()
        move(item, right, left, left_send, right_recv).wait_recv()
        if item not in RELAY_RIGHT:
            move(item, right, left, hop_send, hop_recv).start()

    def far_item(item):
        move(item, far, right, hop_send, hop_recv).wait_recv()

    for j in range(5):
        to_mate(j).start()

    dealt, by_slot = owner_tables(own_ref, spans_ref, adm_ref, perm_ref)
    by_req = dealt.T.astype(BF16)
    dealt = dealt.astype(BF16)
    long_own = fact(by_slot, 0, 2 * g) > 0.5
    sent = nt(dealt, p0_ref[...])
    wide_ref[...] = jnp.zeros_like(wide_ref)
    wide_ref[pl.ds(0, 64, stride=8), 0:16] = sent[0:64]
    wide_ref[pl.ds(1, 64, stride=8), 0:16] = sent[64:128]
    pbuf[...] = wide_ref[0:512, :].astype(BF16).reshape(64, 8, 128)
    pgot[g] = pbuf[g]

    to_mate(0).wait_recv()
    pg[t, 0:HALF, :] = jnp.where(long_own, part_ref[pl.ds(mine, HALF), :], pin[...])
    give(0)
    for j in range(4):
        to_mate(1 + j).wait_recv()
        rows = pl.ds(j * PIECE, PIECE)
        xg[t, rows, :] = jnp.where(long_own, xv_ref[pl.ds(mine + j * PIECE, PIECE), :], xin[rows, :])
        give(1 + j)
        if j == 0:
            scatter_rep(pbuf, pgot, p_send, p_recv, g, t)
    to_mate(5).start()
    to_mate(6).start()

    for c in range(8):
        rows = mm(dealt, km_ref[pl.ds(c, 128, stride=8), :].astype(BF16))
        wide_ref[pl.ds(c, 64, stride=16), :] = rows[0:64]
        wide_ref[pl.ds(8 + c, 64, stride=16), :] = rows[64:128]
    sbuf[...] = wide_ref[...].astype(BF16).reshape(64, 16, 128)
    sgot[g] = sbuf[g]
    scatter_rep(sbuf, sgot, st_send, st_recv, g, t)

    spread = (iota((128, WID), 1) // SPAN == iota((128, WID), 0)).astype(BF16)
    own_lane = iota((64, WID), 1) % SPAN == iota((64, WID), 0)
    row16 = iota((16, WID), 0)
    wait_rep(pgot, p_recv)
    wide_ref[0:512, :] = pgot[...].reshape(512, 128).astype(F32)
    before = []
    for s in range(2):
        vals = mm(wide_ref[pl.ds(s, 64, stride=8), :].astype(BF16), spread)
        before.append(jnp.sum(jnp.where(own_lane, vals, 0.0), axis=0, keepdims=True))
    final = x_ref[TAIL - 16 : TAIL, :].astype(F32)[15:16]
    firsts = [jnp.where(long_own, final, before[0]), before[1]]
    first_ref[...] = jnp.where(iota((8, WID), 0) == 0, firsts[0], firsts[1])
    cur = [x_ref[0:16, :].astype(F32), gx_ref[0:16, :].astype(F32), gx_ref[16:32, :].astype(F32)]
    ahead = [jnp.where(row16 == 0, f, pltpu.roll(x, 1, 0)) for x, f in zip(cur, before[:1] + firsts)]
    zsend[...] = mixed(cur[0], ahead[0], mc).astype(BF16)
    zpart[...] = mm(mixed(cur[0], ahead[0], mf).astype(BF16), sh_ref[...]).astype(BF16)
    to_mate(7).start()
    to_mate(8).start()
    for s in range(2):
        at = HALF + 16 * s
        xg[t, at : at + 16, :] = mixed(cur[1 + s], ahead[1 + s], mc).astype(BF16)
        pg[t, at : at + 16, :] = mm(mixed(cur[1 + s], ahead[1 + s], mf).astype(BF16), sh_ref[...]).astype(BF16)
    hand_on(0)
    hand_on(1)
    to_mate(7).wait_recv()
    to_mate(8).wait_recv()
    at = HALF + 32
    xg[t, at : at + 16, :] = jnp.where(long_own, zsend[...], zin[...])
    pg[t, at : at + 16, :] = jnp.where(long_own, zpart[...], zpin[...])
    for item in range(5, 8):
        give(item)

    def product(source, add):
        def tile(n, _):
            c = pl.ds(pl.multiple_of(n * 256, 256), 256)
            out = mm(xg[source], w_ref[pl.ds(pl.multiple_of(source * WID, WID), WID), c])
            acc[:, c] = acc[:, c] + out if add else out
            return 0

        lax.fori_loop(0, WID // 256, tile, 0)

    for k in range(TP):
        w_copy(k).wait()
    product(t, False)
    hand_on(2)

    counts = []
    wide_ref[0:512, :] = jnp.zeros((512, 128), F32)
    for s in range(2):
        count = fact(by_slot, 1, 2 * g + s).astype(jnp.int32)
        counts.append(count)
        rows = gx_ref[DRAFT * s : DRAFT * s + DRAFT, :].astype(F32)
        edge = jnp.sum(jnp.where(row16 == count - 1, rows, 0.0), axis=0, keepdims=True)
        edge = jnp.where(count > 0, edge, first_ref[s : s + 1, :])
        wide_ref[pl.ds(s, 64, stride=8), :] = nt(jnp.where(own_lane, edge, 0.0).astype(BF16), spread)
    ebuf[...] = wide_ref[0:512, :].astype(BF16).reshape(64, 8, 128)
    egot[g] = ebuf[g]
    hand_on(3)
    hand_on(4)

    wait_rep(sgot, st_recv)
    wide_ref[...] = sgot[...].reshape(1024, 128).astype(F32)
    for p in range(PAIRS):
        st0_ref[p] = wide_ref[pl.ds(p, 64, stride=16), :].astype(BF16)
    to_mate(11).start()

    for item in range(5, 8):
        hand_on(item)
    far_item(0)
    far_item(7)
    low = jnp.tanh(pg[0].astype(F32) + pg[1].astype(F32) + pg[2].astype(F32) + pg[3].astype(F32)).astype(BF16)
    lh[...] = low[0:HALF]
    ll_ref[...] = low[HALF:ROWS]
    swap = (iota((16, RANK), 0) == 0) & (core == 0)
    lh[0:16, :] = jnp.where(swap, ll_ref[32:33, :], lh[0:16, :])
    to_mate(9).start()
    lt_ref[pl.ds(mine, HALF), :] = lh[...]
    scatter_rep(ebuf, egot, e_send, e_recv, g, t)
    product(left, True)
    to_mate(5).wait_recv()
    to_mate(6).wait_recv()
    to_mate(9).wait_recv()

    same = iota((128, 128), 0) // SPAN == iota((128, 128), 1) // SPAN
    heads_sum = same.astype(BF16)
    anchor, boost, scale, shift = anchor_ref[...], boost_ref[...], scale_ref[...], shift_ref[...]

    def ready(i, _):
        rows = pl.ds(pl.multiple_of(i * CHUNK, 16), CHUNK)
        log = -jnp.exp(anchor_ref[:, cols] + mm(lt_ref[rows, :], ex_ref[:, cols]))
        r = jnp.where(long_own, rown[rows, :], rmate[rows, :]).astype(F32)
        k = jnp.where(long_own, kown[rows, :], kmate[rows, :]).astype(F32)
        incl = running(log, CHUNK)
        q, kk, ri = scaled(r, k, incl, log, CHUNK)
        ri_ref[rows, :] = ri
        last = incl[CHUNK - 1 : CHUNK]
        kd = k * jnp.exp(last - incl)
        keep = jnp.exp(last)
        gain = mm(stack((r * boost_ref[:, cols] * k).astype(BF16), SPLIT), heads_sum)
        for p in range(SPLIT):
            c = lanes(p)
            gain_ref[rows, c] = gain[CHUNK * p : CHUNK * p + CHUNK]
            sc_ref[SPLIT * i + p] = scored(q[:, c], kk[:, c], CHUNK)
            kd_ref[SPLIT * i + p] = kd[:, c].T.astype(BF16)
            keep_ref[SPLIT * i + p] = column(keep[:, c])
        return 0

    lax.fori_loop(0, STEPS, ready, 0)
    product(right, True)
    for item in range(1, 7):
        far_item(item)
    product(far, True)
    vh[...] = acc[0:HALF, :].astype(BF16)
    vl_ref[...] = acc[HALF:ROWS, :].astype(BF16)
    vh[0:16, :] = jnp.where((row16 == 0) & (core == 0), vl_ref[32:33, :], vh[0:16, :])
    to_mate(10).start()
    vt_ref[pl.ds(mine, HALF), :] = vh[:, cols]

    for s in range(2):
        rows = slice(DRAFT * s, DRAFT * s + DRAFT)
        log = -jnp.exp(anchor + mm(ll_ref[rows, :], ex_ref[...]))
        r, k, v = gr_ref[rows, :].astype(F32), gk_ref[rows, :].astype(F32), vl_ref[rows, :]
        incl = running(log, DRAFT)
        q, kk, ri = scaled(r, k, incl, log, DRAFT)
        dri_ref[rows, :] = ri
        gain = mm(stack((r * boost * k).astype(BF16), PAIRS), heads_sum)
        taken = row16 < counts[s]
        upto = jnp.sum(jnp.where(taken, log, 0.0), axis=0, keepdims=True)
        weight = jnp.where(taken, jnp.exp(jnp.where(taken, upto - incl, 0.0)), 0.0)
        kd = (k * weight).astype(BF16)
        keep = jnp.exp(upto)
        low16 = iota((DRAFT, 128), 1) < SPAN
        for p in range(PAIRS):
            c = lanes(p)
            both = mm(scored(q[:, c], kk[:, c], DRAFT), v[:, c])
            inner = jnp.where(low16, both[0:DRAFT], both[DRAFT : 2 * DRAFT])
            dy_ref[s, DRAFT * p : DRAFT * p + DRAFT, :] = (
                inner + gain[DRAFT * p : DRAFT * p + DRAFT] * v[:, c].astype(F32)
            )
            du_ref[s, p] = jnp.where(same, tn(kd[:, c], v[:, c]), 0.0)
            dk_ref[s, p] = column(keep[:, c])

    def drafted(s, states):
        rows = slice(DRAFT * s, DRAFT * s + DRAFT)
        y = dy_ref[s] + jnp.concatenate(
            [mm(dri_ref[rows, lanes(p)], states[p].astype(BF16)) for p in range(PAIRS)], axis=0
        )
        for p in range(PAIRS):
            end = states[p] * dk_ref[s, p] + du_ref[s, p]
            wide_ref[pl.ds(512 * s + p, 64, stride=8), :] = end[0:64] + end[64:128]
        rbuf[s] = wide_ref[512 * s : 512 * s + 512, :].astype(BF16).reshape(64, 8, 128)
        rgot[s, g] = rbuf[s, g]
        scatter_rep(rbuf.at[s], rgot.at[s], b_send.at[s], b_recv.at[s], g, t)
        draft_ref[rows, :] = normed(y, heads_sum, scale, shift, DRAFT, PAIRS).astype(BF16)

    late_states = [halves(wide_ref[pl.ds(8 + p, 64, stride=16), :]) for p in range(PAIRS)]
    for p in range(PAIRS):
        dk_ref[2, p] = late_states[p]
    drafted(1, [dk_ref[2, p] for p in range(PAIRS)])

    to_mate(11).wait_recv()
    for p in range(SPLIT):
        start = jnp.where(long_own, st0_ref[core * SPLIT + p], stm_ref[p])
        st_ref[p] = halves(start.astype(F32))
    to_mate(10).wait_recv()
    low32 = iota((CHUNK, 128), 1) < SPAN

    def step(i, _):
        rows = pl.ds(pl.multiple_of(i * CHUNK, 16), CHUNK)
        for p in range(SPLIT):
            c = lanes(p)
            v = vt_ref[rows, c]
            both = mm(sc_ref[SPLIT * i + p], v)
            state = st_ref[p]
            y = jnp.where(low32, both[0:CHUNK], both[CHUNK : 2 * CHUNK])
            y_ref[rows, c] = y + mm(ri_ref[rows, c], state.astype(BF16)) + gain_ref[rows, c] * v.astype(F32)
            st_ref[p] = state * keep_ref[SPLIT * i + p] + jnp.where(same, mm(kd_ref[SPLIT * i + p], v), 0.0)
        return 0

    lax.fori_loop(0, STEPS, step, 0, unroll=3)
    to_mate(12).start()

    to_mate(12).wait_recv()
    states = []
    for p in range(PAIRS):
        here = core == p // SPLIT
        end = jnp.where(here, st_ref[p % SPLIT], endm_ref[p % SPLIT])
        states.append(jnp.where(long_own, end, halves(st0_ref[p].astype(F32))))
    for p in range(PAIRS):
        dk_ref[2, p] = states[p]
    drafted(0, [dk_ref[2, p] for p in range(PAIRS)])

    def finish(i, _):
        rows = pl.ds(pl.multiple_of(i * CHUNK, 16), CHUNK)
        y = stack(y_ref[rows, :], SPLIT)
        o_ref[rows, :] = normed(y, heads_sum, scale_ref[:, cols], shift_ref[:, cols], CHUNK, SPLIT).astype(BF16)
        return 0

    lax.fori_loop(0, STEPS, finish, 0)
    to_mate(13).start()
    tail_ref[:, cols] = jnp.where(long_own, o_ref[...], jnp.zeros((TAIL, SIDE), BF16))

    wait_rep(egot, e_recv)
    wide_ref[0:512, :] = egot[...].reshape(512, 128).astype(F32)
    edges = jnp.concatenate([wide_ref[pl.ds(0, 64, stride=8), :], wide_ref[pl.ds(1, 64, stride=8), :]], axis=0)
    prior_ref[...] = tn(edges.astype(BF16), dealt)[0:16].astype(BF16)
    to_mate(13).wait_recv()
    tail_ref[:, mate_cols] = jnp.where(long_own, om_ref[...], jnp.zeros((TAIL, SIDE), BF16))
    for s in range(2):
        wait_rep(rgot.at[s], b_recv.at[s])
    wide_ref[...] = rgot[...].reshape(1024, 128).astype(F32)
    for c in range(8):
        rows = jnp.concatenate(
            [wide_ref[pl.ds(c, 64, stride=8), :], wide_ref[pl.ds(512 + c, 64, stride=8), :]], axis=0
        )
        state_ref[pl.ds(c, 128, stride=8), :] = mm(by_req, rows.astype(BF16))

    wait_rep(pbuf, p_send)
    wait_rep(sbuf, st_send)
    wait_rep(ebuf, e_send)
    for s in range(2):
        wait_rep(rbuf.at[s], b_send.at[s])
    for j in range(14):
        to_mate(j).wait_send()
    for item in range(8):
        move(item, t, right, right_send, left_recv).wait_send()
        move(item, t, left, left_send, right_recv).wait_send()
        move(item, far, right, hop_send, hop_recv).wait_send()


def place_kernel(a_ref, b_ref, c_ref, d_ref, a_out, b_out, c_out, d_out, sem):
    pairs = ((a_ref, a_out), (b_ref, b_out), (c_ref, c_out), (d_ref, d_out))
    copies = [pltpu.make_async_copy(src, dst, sem.at[i]) for i, (src, dst) in enumerate(pairs)]
    for c in copies:
        c.start()
    for c in copies:
        c.wait()


VM = pl.BlockSpec(memory_space=pltpu.VMEM)
ANY = pl.BlockSpec(memory_space=pl.ANY)
DMA = pltpu.SemaphoreType.DMA


def local(
    suffix_source, suffix_accept, suffix_address, guess_lane_source, guess_lane_accept, guess_lane_address,
    content_map, forget_shrink_map, forget_expand_map, forget_lane_anchor, present_boost,
    content_blend_share, forget_blend_share, lane_normal_scale, lane_normal_shift,
    kernel_memory_saved, prior_source_saved, lane_owner, request_spans, admitted_guesses,
):
    small = [a.reshape(1, 128) for a in (lane_owner, request_spans, admitted_guesses)]
    chan = [
        a.reshape(1, WID)
        for a in (forget_lane_anchor, present_boost, lane_normal_scale, lane_normal_shift)
    ]
    sds = jax.ShapeDtypeStruct
    shapes = (
        sds((TAIL, WID), BF16),
        sds((2 * DRAFT, WID), BF16),
        sds((1024, 128), F32),
        sds((16, 128), BF16),
    )
    vm = pltpu.VMEM
    row, ints, drafts = vm((1, WID), F32), vm((1, 128), jnp.int32), vm((2 * DRAFT, WID), BF16)
    side, tile16, tile8 = vm((TAIL, SIDE), BF16), vm((REP, 16, 128), BF16), vm((REP, 8, 128), BF16)
    outs = pl.pallas_call(
        mix_kernel,
        name="time_mix",
        out_shape=shapes,
        in_specs=[ANY] * 20,
        out_specs=(VM,) * 4,
        scratch_shapes=[
            vm((TAIL, WID), BF16), drafts, vm((1024, 128), F32), vm((16, 128), BF16), row, row,
            ints, ints, ints, drafts, drafts, vm((RANK, WID), BF16), row, row, row, row,
            vm((TP * WID, WID), BF16), vm((WID, RANK), BF16), side, side,
            vm((128, 128), F32), vm((1024, 128), F32), tile16, tile16, tile8, tile8,
            vm((TAIL, WID), BF16), vm((TAIL, RANK), BF16), vm((HALF, WID), BF16), vm((HALF, RANK), BF16),
            vm((16, WID), BF16), vm((16, RANK), BF16), vm((16, WID), BF16), vm((16, RANK), BF16),
            vm((TP, ROWS, WID), BF16), vm((TP, ROWS, RANK), BF16), vm((ROWS, WID), F32),
            vm((HALF, WID), BF16), vm((HALF, RANK), BF16), vm((LATE, WID), BF16), vm((LATE, RANK), BF16),
            vm((8, WID), F32), side, vm((TAIL, RANK), BF16), side, side,
            vm((PAIRS, 64, 128), BF16), vm((SPLIT, 64, 128), BF16),
            vm((STEPS * SPLIT, 2 * CHUNK, CHUNK), BF16), side, vm((TAIL, SIDE), F32),
            vm((STEPS * SPLIT, 128, CHUNK), BF16), vm((STEPS * SPLIT, 128, 128), F32),
            vm((SPLIT, 128, 128), F32), vm((SPLIT, 128, 128), F32), vm((TAIL, SIDE), F32), side, side,
            vm((2, 128, 128), F32), drafts, vm((2, PAIRS, 128, 128), F32), vm((3, PAIRS, 128, 128), F32),
            vm((2, REP, 8, 128), BF16), vm((2, REP, 8, 128), BF16), tile8, tile8,
            DMA((19,)), DMA((TP,)), DMA, DMA, DMA, DMA, DMA, DMA, DMA((2,)), DMA((2,)), DMA((14,)), DMA((14,)),
            DMA((8,)), DMA((8,)), DMA((8,)), DMA((8,)), DMA((8,)), DMA((8,)),
        ],
        compiler_params=pltpu.CompilerParams(
            collective_id=0, has_side_effects=True, vmem_limit_bytes=56 << 20
        ),
    )(
        suffix_source.reshape(TAIL, WID),
        guess_lane_source.reshape(2 * DRAFT, WID),
        kernel_memory_saved.reshape(1024, 128),
        prior_source_saved.reshape(128, 16).T,
        content_blend_share.reshape(1, WID),
        forget_blend_share.reshape(1, WID),
        *small,
        guess_lane_accept.reshape(2 * DRAFT, WID),
        guess_lane_address.reshape(2 * DRAFT, WID),
        forget_expand_map,
        *chan,
        content_map,
        forget_shrink_map,
        suffix_accept.reshape(TAIL, WID),
        suffix_address.reshape(TAIL, WID),
    )
    tail, draft, state, prior = pl.pallas_call(
        place_kernel,
        name="place",
        out_shape=shapes,
        in_specs=[VM] * 4,
        out_specs=(ANY,) * 4,
        scratch_shapes=[DMA((4,))],
    )(*outs)
    return (
        tail.reshape(1, TAIL, WID),
        draft.reshape(2, DRAFT, WID),
        state.reshape(128, 1, WID),
        prior.T.reshape(128, 1, 16),
    )


def solution(mesh):
    rows, cols, chan = P("rep", None, "tp"), P(None, "tp"), P("tp")
    cache = P(None, "rep", "tp")
    return jax.shard_map(
        local,
        mesh=mesh,
        in_specs=(rows,) * 6 + (cols, P(), cols) + (chan,) * 6 + (cache, cache, P(), P(), P()),
        out_specs=(rows, rows, cache, cache),
        check_vma=False,
    )
```

```python
import jax
import jax.numpy as jnp
from jax import lax
from jax.experimental import pallas as pl
from jax.experimental.pallas import tpu as pltpu
from jax.sharding import PartitionSpec as P

SPAN = 64
DRAFT = 16
EPS = 0.00064
REP = 64
ROW = 8
TP = 4
WID = 1024
TAIL = 384
HALF = 192
LATE = 48
ROWS = HALF + LATE
PIECE = 48
CHUNK = 32
PAIRS = 8
RANK = 128
F32 = jnp.float32
BF16 = jnp.bfloat16
MESH = pl.DeviceIdType.MESH

SIDE = WID // 2
SPLIT = PAIRS // 2
STEPS = TAIL // CHUNK

ITEMS = (
    ("p", 0, 192),
    ("x", 0, 48),
    ("x", 48, 48),
    ("x", 96, 48),
    ("x", 144, 48),
    ("x", 192, 16),
    ("x", 208, 32),
    ("p", 192, 48),
)
RELAY_RIGHT = (1, 3, 5)
DIRECT = (0, 7)


def iota(shape, dim):
    return lax.broadcasted_iota(jnp.int32, shape, dim)


def nt(a, b):
    return lax.dot_general(a, b, (((1,), (1,)), ((), ())), preferred_element_type=F32)


def tn(a, b):
    return lax.dot_general(a, b, (((0,), (0,)), ((), ())), preferred_element_type=F32)


def mm(a, b):
    return jnp.dot(a, b, preferred_element_type=F32)


def owner_tables(own_ref, spans_ref, adm_ref, perm_ref):
    hot = (iota((128, 128), 0) == own_ref[...]).astype(F32)
    row = iota((8, 128), 0)
    long_q = (spans_ref[...] > DRAFT).astype(F32)
    facts = jnp.where(row == 0, long_q, jnp.where(row == 1, adm_ref[...].astype(F32), 0.0))
    by_slot = mm(facts.astype(BF16), hot.astype(BF16))
    perm_ref[...] = hot.T
    dealt = jnp.concatenate([perm_ref[pl.ds(0, 64, stride=2), :], perm_ref[pl.ds(1, 64, stride=2), :]], axis=0)
    return dealt, by_slot


def fact(by_slot, row, slot):
    pick = iota((8, 128), 1) == slot
    here = jnp.where(pick & (iota((8, 128), 0) == row), by_slot, 0.0)
    return jnp.sum(jnp.sum(here, axis=1, keepdims=True), axis=0, keepdims=True)


def greet_near(barrier, g, t):
    near = [(g, lax.rem(t + d, TP)) for d in range(1, TP)]
    near += [(g - lax.rem(g, ROW) + lax.rem(g + d, ROW), t) for d in range(1, ROW)]
    near += [(lax.rem(g + ROW * d, REP), t) for d in (1, 2, 6, 7)]
    for to in near:
        pl.semaphore_signal(barrier, inc=1, device_id=to, device_id_type=MESH)
    return len(near)


def pass_on(sem, g, t, steps):
    for d in steps:
        pl.semaphore_signal(sem, inc=1, device_id=(lax.rem(g + ROW * d, REP), t), device_id_type=MESH)


def scatter_rep(src, dst, send, recv, g, t):
    def one(d, _):
        to = lax.rem(g + d, REP)
        pltpu.make_async_remote_copy(
            src_ref=src.at[to],
            dst_ref=dst.at[g],
            send_sem=send,
            recv_sem=recv,
            device_id=(to, t),
            device_id_type=MESH,
        ).start()
        return 0

    lax.fori_loop(1, REP, one, 0, unroll=7)


def wait_rep(buf, sem):
    part = buf.at[pl.ds(0, REP - 1)]
    pltpu.make_async_copy(part, part, sem).wait()


def mixed(x, prev, share):
    return x + (prev - x) * share


def halves(a):
    low = iota(a.shape, 1) < SPAN
    zero = jnp.zeros_like(a)
    return jnp.concatenate([jnp.where(low, a, zero), jnp.where(low, zero, a)], axis=0)


def lanes(p):
    return slice(128 * p, 128 * p + 128)


def stack(a, pairs):
    return jnp.concatenate([a[:, lanes(p)] for p in range(pairs)], axis=0)


def running(log, n):
    tri = (iota((n, n), 0) >= iota((n, n), 1)).astype(BF16)
    hi = log.astype(BF16)
    lo = (log - hi.astype(F32)).astype(BF16)
    return mm(tri, hi) + mm(tri, lo)


def column(row):
    hi = row.astype(BF16).astype(F32)
    rest = row - hi
    mid = rest.astype(BF16).astype(F32)
    low = rest - mid
    at = iota((16, 128), 0)
    parts = jnp.where(at == 0, hi, jnp.where(at == 1, mid, jnp.where(at == 2, low, 0.0)))
    return tn(parts.astype(BF16), jnp.ones((16, 128), BF16))


def scaled(r, k, incl, log, n):
    excl = incl - log
    mid = incl[n // 2 : n // 2 + 1]
    q = (r * jnp.exp(jnp.minimum(excl - mid, 80.0))).astype(BF16)
    kk = (k * jnp.exp(jnp.minimum(mid - incl, 80.0))).astype(BF16)
    return q, kk, (r * jnp.exp(excl)).astype(BF16)


def scored(q, kk, n):
    strict = iota((2 * n, n), 0) % n > iota((2 * n, n), 1)
    return jnp.where(strict, nt(halves(q), kk), 0.0).astype(BF16)


def normed(y, heads_sum, scale, shift, n, pairs):
    hi = y.astype(BF16)
    lo = (y - hi.astype(F32)).astype(BF16)
    center = y - (mm(hi, heads_sum) + mm(lo, heads_sum)) * (1.0 / SPAN)
    spread = mm((center * center).astype(BF16), heads_sum) * (1.0 / SPAN)
    o = center * lax.rsqrt(spread + EPS)
    return jnp.concatenate(
        [o[n * p : n * p + n] * scale[:, lanes(p)] + shift[:, lanes(p)] for p in range(pairs)], axis=1
    )


def mix_kernel(
    x_hbm, gx_hbm, km_hbm, p0_hbm, mc_hbm, mf_hbm, own_hbm, spans_hbm, adm_hbm, gr_hbm, gk_hbm, ex_hbm,
    anchor_hbm, boost_hbm, scale_hbm, shift_hbm, w_hbm, sh_hbm, rt_hbm, kt_hbm,
    tail_ref, draft_ref, state_ref, prior_ref,
    x_ref, gx_ref, km_ref, p0_ref, mc_ref, mf_ref, own_ref, spans_ref, adm_ref, gr_ref, gk_ref, ex_ref,
    anchor_ref, boost_ref, scale_ref, shift_ref, w_ref, sh_ref, rown, kown,
    perm_ref, wide_ref, sbuf, sgot, pbuf, pgot, xv_ref, part_ref, xin, pin, zsend, zpart, zin, zpin,
    xg, pg, acc, vh, lh, vl_ref, ll_ref, vt_ref, lt_ref, rmate, kmate, st0_ref, stm_ref,
    sc_ref, ri_ref, gain_ref, kd_ref, keep_ref, st_ref, endm_ref, y_ref, o_ref, om_ref,
    dy_ref, dri_ref, du_ref, dk_ref, rbuf, rgot, ebuf, egot, lz_ref,
    in_sem, w_sem, st_send, st_recv, p_send, p_recv, e_send, e_recv, b_send, b_recv, mate_send, mate_recv,
    right_send, left_recv, left_send, right_recv, hop_send, hop_recv, round1, round2,
):
    g, t = lax.axis_index("rep"), lax.axis_index("tp")
    core = lax.rem(g, 2)
    mate = g + 1 - 2 * core
    right, left, far = lax.rem(t + 1, TP), lax.rem(t + 3, TP), lax.rem(t + 2, TP)
    mine = pl.multiple_of(core * HALF, 16)
    other = pl.multiple_of((1 - core) * HALF, 16)
    cols = pl.ds(pl.multiple_of(core * SIDE, 128), SIDE)
    mate_cols = pl.ds(pl.multiple_of((1 - core) * SIDE, 128), SIDE)

    own_rows = pl.ds(pl.multiple_of(t * WID, WID), WID)
    plain = (
        (x_hbm, x_ref), (mf_hbm, mf_ref), (mc_hbm, mc_ref), (sh_hbm.at[own_rows], sh_ref), (own_hbm, own_ref),
        (spans_hbm, spans_ref), (adm_hbm, adm_ref), (p0_hbm, p0_ref), (gx_hbm, gx_ref), (km_hbm, km_ref),
        (rt_hbm.at[:, cols], rown), (kt_hbm.at[:, cols], kown), (gr_hbm, gr_ref), (gk_hbm, gk_ref), (ex_hbm, ex_ref),
        (anchor_hbm, anchor_ref), (boost_hbm, boost_ref), (scale_hbm, scale_ref), (shift_hbm, shift_ref),
    )

    def in_copy(i):
        return pltpu.make_async_copy(plain[i][0], plain[i][1], in_sem.at[i])

    def w_copy(k):
        rows = pl.ds(k * WID, WID)
        return pltpu.make_async_copy(w_hbm.at[rows], w_ref.at[rows], w_sem.at[k])

    for i in range(len(plain)):
        in_copy(i).start()
    for k in range(TP):
        w_copy(k).start()

    barrier = pltpu.get_barrier_semaphore()
    greeted = greet_near(barrier, g, t)

    for i in range(4):
        in_copy(i).wait()
    mc, mf = mc_ref[...], mf_ref[...]

    def mix_rows(j, _):
        r0 = pl.multiple_of(j * PIECE, 16)
        x = x_ref[pl.ds(r0, PIECE), :].astype(F32)
        ahead = x_ref[pl.ds(pl.multiple_of(jnp.maximum(r0 - 16, 0), 16), 16), :].astype(F32)
        prev = jnp.where(iota((PIECE, WID), 0) == 0, ahead[15:16], pltpu.roll(x, 1, 0))
        xv_ref[pl.ds(r0, PIECE), :] = mixed(x, prev, mc).astype(BF16)
        part_ref[pl.ds(r0, PIECE), :] = mm(mixed(x, prev, mf).astype(BF16), sh_ref[...]).astype(BF16)
        return 0

    lax.fori_loop(0, TAIL // PIECE, mix_rows, 0)
    for i in range(4, len(plain)):
        in_copy(i).wait()
    pl.semaphore_wait(barrier, greeted)
    pass_on(round1, g, t, (1, 2, 6, 7))

    moves = {
        0: (part_ref.at[pl.ds(other, HALF)], pin),
        5: (rt_hbm.at[:, mate_cols], rmate),
        6: (kt_hbm.at[:, mate_cols], kmate),
        7: (zsend, zin),
        8: (zpart, zpin),
        9: (lh, lt_ref.at[pl.ds(mine, HALF)]),
        10: (vh.at[:, mate_cols], vt_ref.at[pl.ds(mine, HALF)]),
        11: (st0_ref.at[pl.ds((1 - core) * SPLIT, SPLIT)], stm_ref),
        12: (st_ref, endm_ref),
        13: (o_ref, om_ref),
        14: (ll_ref.at[pl.ds(32, 16)], lz_ref),
    }
    for j in range(4):
        moves[1 + j] = (xv_ref.at[pl.ds(other + j * PIECE, PIECE)], xin.at[pl.ds(j * PIECE, PIECE)])

    def to_mate(j):
        return pltpu.make_async_remote_copy(
            src_ref=moves[j][0],
            dst_ref=moves[j][1],
            send_sem=mate_send.at[j],
            recv_sem=mate_recv.at[j],
            device_id=(mate, t),
            device_id_type=MESH,
        )

    def part_of(item, source):
        kind, r0, n = ITEMS[item]
        return (xg if kind == "x" else pg).at[source, pl.ds(r0, n)]

    def move(item, source, to, send, recv):
        return pltpu.make_async_remote_copy(
            src_ref=part_of(item, source),
            dst_ref=part_of(item, source),
            send_sem=send.at[item],
            recv_sem=recv.at[item],
            device_id=(g, to),
            device_id_type=MESH,
        )

    def give(item):
        move(item, t, right, right_send, left_recv).start()
        move(item, t, left, left_send, right_recv).start()
        if item in DIRECT:
            move(item, t, far, hop_send, hop_recv).start()

    def hand_on(item):
        move(item, left, right, right_send, left_recv).wait_recv()
        if item in RELAY_RIGHT:
            move(item, left, right, hop_send, hop_recv).start()
        move(item, right, left, left_send, right_recv).wait_recv()
        if item not in RELAY_RIGHT + DIRECT:
            move(item, right, left, hop_send, hop_recv).start()

    def far_item(item):
        move(item, far, right, hop_send, hop_recv).wait_recv()

    for j in range(5):
        to_mate(j).start()

    dealt, by_slot = owner_tables(own_ref, spans_ref, adm_ref, perm_ref)
    by_req = dealt.T.astype(BF16)
    dealt = dealt.astype(BF16)
    long_own = fact(by_slot, 0, 2 * g) > 0.5
    sent = nt(dealt, p0_ref[...])
    wide_ref[...] = jnp.zeros_like(wide_ref)
    wide_ref[pl.ds(0, 64, stride=8), 0:16] = sent[0:64]
    wide_ref[pl.ds(1, 64, stride=8), 0:16] = sent[64:128]
    pbuf[...] = wide_ref[0:512, :].astype(BF16).reshape(64, 8, 128)
    pgot[g] = pbuf[g]

    to_mate(0).wait_recv()
    pg[t, 0:HALF, :] = jnp.where(long_own, part_ref[pl.ds(mine, HALF), :], pin[...])
    give(0)
    for j in range(4):
        to_mate(1 + j).wait_recv()
        rows = pl.ds(j * PIECE, PIECE)
        xg[t, rows, :] = jnp.where(long_own, xv_ref[pl.ds(mine + j * PIECE, PIECE), :], xin[rows, :])
        give(1 + j)
        if j == 1:
            pl.semaphore_wait(round1, 4)
            pass_on(round2, g, t, (3, 4, 5))
    to_mate(5).start()
    to_mate(6).start()

    hand_on(0)
    far_item(0)

    def low_rank(r0, n):
        parts = [pg[k, r0 : r0 + n, :].astype(F32) for k in range(TP)]
        return jnp.tanh(parts[0] + parts[1] + parts[2] + parts[3]).astype(BF16)

    lh[...] = low_rank(0, HALF)
    to_mate(9).start()
    lt_ref[pl.ds(mine, HALF), :] = lh[...]
    pl.semaphore_wait(round2, 3)
    scatter_rep(pbuf, pgot, p_send, p_recv, g, t)
    hand_on(1)

    for c in range(8):
        rows = mm(dealt, km_ref[pl.ds(c, 128, stride=8), :].astype(BF16))
        wide_ref[pl.ds(c, 64, stride=16), :] = rows[0:64]
        wide_ref[pl.ds(8 + c, 64, stride=16), :] = rows[64:128]
    sbuf[...] = wide_ref[...].astype(BF16).reshape(64, 16, 128)
    sgot[g] = sbuf[g]
    scatter_rep(sbuf, sgot, st_send, st_recv, g, t)
    hand_on(2)

    same = iota((128, 128), 0) // SPAN == iota((128, 128), 1) // SPAN
    heads_sum = same.astype(BF16)
    anchor, boost, scale, shift = anchor_ref[...], boost_ref[...], scale_ref[...], shift_ref[...]

    def ready(i, _):
        rows = pl.ds(pl.multiple_of(i * CHUNK, 16), CHUNK)
        log = -jnp.exp(anchor_ref[:, cols] + mm(lt_ref[rows, :], ex_ref[:, cols]))
        r = jnp.where(long_own, rown[rows, :], rmate[rows, :]).astype(F32)
        k = jnp.where(long_own, kown[rows, :], kmate[rows, :]).astype(F32)
        incl = running(log, CHUNK)
        q, kk, ri = scaled(r, k, incl, log, CHUNK)
        ri_ref[rows, :] = ri
        last = incl[CHUNK - 1 : CHUNK]
        kd = k * jnp.exp(last - incl)
        keep = jnp.exp(last)
        gain = mm(stack((r * boost_ref[:, cols] * k).astype(BF16), SPLIT), heads_sum)
        for p in range(SPLIT):
            c = lanes(p)
            gain_ref[rows, c] = gain[CHUNK * p : CHUNK * p + CHUNK]
            sc_ref[SPLIT * i + p] = scored(q[:, c], kk[:, c], CHUNK)
            kd_ref[SPLIT * i + p] = kd[:, c].T.astype(BF16)
            keep_ref[SPLIT * i + p] = column(keep[:, c])
        return 0

    def product(source, add):
        def tile(n, _):
            c = pl.ds(pl.multiple_of(n * 256, 256), 256)
            out = mm(xg[source], w_ref[pl.ds(pl.multiple_of(source * WID, WID), WID), c])
            acc[:, c] = acc[:, c] + out if add else out
            return 0

        lax.fori_loop(0, WID // 256, tile, 0)

    to_mate(5).wait_recv()
    to_mate(6).wait_recv()
    to_mate(9).wait_recv()

    spread = (iota((128, WID), 1) // SPAN == iota((128, WID), 0)).astype(BF16)
    own_lane = iota((64, WID), 1) % SPAN == iota((64, WID), 0)
    row16 = iota((16, WID), 0)
    firsts = []

    def late_rows():
        wait_rep(pgot, p_recv)
        wide_ref[0:512, :] = pgot[...].reshape(512, 128).astype(F32)
        before = []
        for s in range(2):
            vals = mm(wide_ref[pl.ds(s, 64, stride=8), :].astype(BF16), spread)
            before.append(jnp.sum(jnp.where(own_lane, vals, 0.0), axis=0, keepdims=True))
        final = x_ref[TAIL - 16 : TAIL, :].astype(F32)[15:16]
        firsts.extend([jnp.where(long_own, final, before[0]), before[1]])
        cur = [x_ref[0:16, :].astype(F32), gx_ref[0:16, :].astype(F32), gx_ref[16:32, :].astype(F32)]
        ahead = [jnp.where(row16 == 0, f, pltpu.roll(x, 1, 0)) for x, f in zip(cur, before[:1] + firsts)]
        zsend[...] = mixed(cur[0], ahead[0], mc).astype(BF16)
        zpart[...] = mm(mixed(cur[0], ahead[0], mf).astype(BF16), sh_ref[...]).astype(BF16)
        to_mate(7).start()
        to_mate(8).start()
        for s in range(2):
            at = HALF + 16 * s
            xg[t, at : at + 16, :] = mixed(cur[1 + s], ahead[1 + s], mc).astype(BF16)
            pg[t, at : at + 16, :] = mm(mixed(cur[1 + s], ahead[1 + s], mf).astype(BF16), sh_ref[...]).astype(BF16)

    def give_late():
        to_mate(7).wait_recv()
        to_mate(8).wait_recv()
        at = HALF + 32
        xg[t, at : at + 16, :] = jnp.where(long_own, zsend[...], zin[...])
        pg[t, at : at + 16, :] = jnp.where(long_own, zpart[...], zpin[...])
        for item in (7, 5, 6):
            give(item)

    counts = []

    def edges_out():
        wide_ref[0:512, :] = jnp.zeros((512, 128), F32)
        for s in range(2):
            count = fact(by_slot, 1, 2 * g + s).astype(jnp.int32)
            counts.append(count)
            rows = gx_ref[DRAFT * s : DRAFT * s + DRAFT, :].astype(F32)
            edge = jnp.sum(jnp.where(row16 == count - 1, rows, 0.0), axis=0, keepdims=True)
            edge = jnp.where(count > 0, edge, firsts[s])
            wide_ref[pl.ds(s, 64, stride=8), :] = nt(jnp.where(own_lane, edge, 0.0).astype(BF16), spread)
        ebuf[...] = wide_ref[0:512, :].astype(BF16).reshape(64, 8, 128)
        egot[g] = ebuf[g]
        scatter_rep(ebuf, egot, e_send, e_recv, g, t)

    lax.fori_loop(1, 4, ready, 0)
    hand_on(3)
    late_rows()
    hand_on(4)
    lax.fori_loop(4, 6, ready, 0)
    give_late()
    edges_out()
    wait_rep(sgot, st_recv)
    wide_ref[...] = sgot[...].reshape(1024, 128).astype(F32)
    for p in range(PAIRS):
        st0_ref[p] = wide_ref[pl.ds(p, 64, stride=16), :].astype(BF16)
    to_mate(11).start()
    for p in range(PAIRS):
        dk_ref[2, p] = halves(wide_ref[pl.ds(8 + p, 64, stride=16), :])
    lax.fori_loop(6, STEPS, ready, 0)
    for k in range(TP):
        w_copy(k).wait()
    hand_on(7)
    far_item(7)
    hand_on(5)
    hand_on(6)
    ll_ref[...] = low_rank(HALF, LATE)
    to_mate(14).start()
    product(t, False)
    product(left, True)
    to_mate(14).wait_recv()
    head = jnp.where(core == 0, ll_ref[32:33, :], lz_ref[0:1, :])
    lt_ref[0:16, :] = jnp.where(iota((16, RANK), 0) == 0, head, lt_ref[0:16, :])
    ready(0, 0)
    product(right, True)
    to_mate(11).wait_recv()
    for p in range(SPLIT):
        start = jnp.where(long_own, st0_ref[core * SPLIT + p], stm_ref[p])
        st_ref[p] = halves(start.astype(F32))
    for item in range(1, 7):
        far_item(item)
    product(far, True)
    vh[...] = acc[0:HALF, :].astype(BF16)
    vl_ref[...] = acc[HALF:ROWS, :].astype(BF16)
    vh[0:16, :] = jnp.where((row16 == 0) & (core == 0), vl_ref[32:33, :], vh[0:16, :])
    to_mate(10).start()
    vt_ref[pl.ds(mine, HALF), :] = vh[:, cols]

    low16 = iota((DRAFT, 128), 1) < SPAN

    def draft_ready(s):
        rows = slice(DRAFT * s, DRAFT * s + DRAFT)
        log = -jnp.exp(anchor + mm(ll_ref[rows, :], ex_ref[...]))
        r, k, v = gr_ref[rows, :].astype(F32), gk_ref[rows, :].astype(F32), vl_ref[rows, :]
        incl = running(log, DRAFT)
        q, kk, ri = scaled(r, k, incl, log, DRAFT)
        dri_ref[rows, :] = ri
        gain = mm(stack((r * boost * k).astype(BF16), PAIRS), heads_sum)
        taken = row16 < counts[s]
        upto = jnp.sum(jnp.where(taken, log, 0.0), axis=0, keepdims=True)
        weight = jnp.where(taken, jnp.exp(jnp.where(taken, upto - incl, 0.0)), 0.0)
        kd = (k * weight).astype(BF16)
        keep = jnp.exp(upto)
        for p in range(PAIRS):
            c = lanes(p)
            both = mm(scored(q[:, c], kk[:, c], DRAFT), v[:, c])
            inner = jnp.where(low16, both[0:DRAFT], both[DRAFT : 2 * DRAFT])
            dy_ref[s, DRAFT * p : DRAFT * p + DRAFT, :] = (
                inner + gain[DRAFT * p : DRAFT * p + DRAFT] * v[:, c].astype(F32)
            )
            du_ref[s, p] = jnp.where(same, tn(kd[:, c], v[:, c]), 0.0)
            dk_ref[s, p] = column(keep[:, c])

    def accept(s, p, state):
        rows = slice(DRAFT * s, DRAFT * s + DRAFT)
        at = slice(DRAFT * p, DRAFT * p + DRAFT)
        dy_ref[s, at, :] = dy_ref[s, at, :] + mm(dri_ref[rows, lanes(p)], state.astype(BF16))
        end = state * dk_ref[s, p] + du_ref[s, p]
        wide_ref[pl.ds(8 * s + p, 64, stride=16), :] = end[0:64] + end[64:128]

    draft_ready(0)

    to_mate(10).wait_recv()
    low32 = iota((CHUNK, 128), 1) < SPAN

    def step(i, _):
        rows = pl.ds(pl.multiple_of(i * CHUNK, 16), CHUNK)
        for p in range(SPLIT):
            c = lanes(p)
            v = vt_ref[rows, c]
            both = mm(sc_ref[SPLIT * i + p], v)
            state = st_ref[p]
            y = jnp.where(low32, both[0:CHUNK], both[CHUNK : 2 * CHUNK])
            y_ref[rows, c] = y + mm(ri_ref[rows, c], state.astype(BF16)) + gain_ref[rows, c] * v.astype(F32)
            st_ref[p] = state * keep_ref[SPLIT * i + p] + jnp.where(same, mm(kd_ref[SPLIT * i + p], v), 0.0)
        return 0

    lax.fori_loop(0, STEPS, step, 0, unroll=3)
    to_mate(12).start()

    draft_ready(1)
    for p in range(PAIRS):
        accept(1, p, dk_ref[2, p])
    to_mate(12).wait_recv()
    for p in range(PAIRS):
        end = jnp.where(core == p // SPLIT, st_ref[p % SPLIT], endm_ref[p % SPLIT])
        accept(0, p, jnp.where(long_own, end, halves(st0_ref[p].astype(F32))))
    rbuf[...] = wide_ref[...].astype(BF16).reshape(64, 16, 128)
    rgot[g] = rbuf[g]
    scatter_rep(rbuf, rgot, b_send, b_recv, g, t)
    for s in range(2):
        draft_ref[DRAFT * s : DRAFT * s + DRAFT, :] = normed(
            dy_ref[s], heads_sum, scale, shift, DRAFT, PAIRS
        ).astype(BF16)

    def finish(i, _):
        rows = pl.ds(pl.multiple_of(i * CHUNK, 16), CHUNK)
        y = stack(y_ref[rows, :], SPLIT)
        o_ref[rows, :] = normed(y, heads_sum, scale_ref[:, cols], shift_ref[:, cols], CHUNK, SPLIT).astype(BF16)
        return 0

    lax.fori_loop(0, STEPS, finish, 0)
    to_mate(13).start()
    tail_ref[:, cols] = jnp.where(long_own, o_ref[...], jnp.zeros((TAIL, SIDE), BF16))

    wait_rep(egot, e_recv)
    wide_ref[0:512, :] = egot[...].reshape(512, 128).astype(F32)
    edges = jnp.concatenate([wide_ref[pl.ds(0, 64, stride=8), :], wide_ref[pl.ds(1, 64, stride=8), :]], axis=0)
    prior_ref[...] = tn(edges.astype(BF16), dealt)[0:16].astype(BF16)
    to_mate(13).wait_recv()
    tail_ref[:, mate_cols] = jnp.where(long_own, om_ref[...], jnp.zeros((TAIL, SIDE), BF16))
    wait_rep(rgot, b_recv)
    wide_ref[...] = rgot[...].reshape(1024, 128).astype(F32)
    for c in range(8):
        rows = jnp.concatenate(
            [wide_ref[pl.ds(c, 64, stride=16), :], wide_ref[pl.ds(8 + c, 64, stride=16), :]], axis=0
        )
        state_ref[pl.ds(c, 128, stride=8), :] = mm(by_req, rows.astype(BF16))

    wait_rep(pbuf, p_send)
    wait_rep(sbuf, st_send)
    wait_rep(ebuf, e_send)
    wait_rep(rbuf, b_send)
    for j in range(15):
        to_mate(j).wait_send()
    for item in range(8):
        move(item, t, right, right_send, left_recv).wait_send()
        move(item, t, left, left_send, right_recv).wait_send()
        move(item, far, right, hop_send, hop_recv).wait_send()


def place_kernel(a_ref, b_ref, c_ref, d_ref, a_out, b_out, c_out, d_out, sem):
    pairs = ((a_ref, a_out), (b_ref, b_out), (c_ref, c_out), (d_ref, d_out))
    copies = [pltpu.make_async_copy(src, dst, sem.at[i]) for i, (src, dst) in enumerate(pairs)]
    for c in copies:
        c.start()
    for c in copies:
        c.wait()


VM = pl.BlockSpec(memory_space=pltpu.VMEM)
ANY = pl.BlockSpec(memory_space=pl.ANY)
DMA = pltpu.SemaphoreType.DMA


def local(
    suffix_source, suffix_accept, suffix_address, guess_lane_source, guess_lane_accept, guess_lane_address,
    content_map, forget_shrink_map, forget_expand_map, forget_lane_anchor, present_boost,
    content_blend_share, forget_blend_share, lane_normal_scale, lane_normal_shift,
    kernel_memory_saved, prior_source_saved, lane_owner, request_spans, admitted_guesses,
):
    small = [a.reshape(1, 128) for a in (lane_owner, request_spans, admitted_guesses)]
    chan = [
        a.reshape(1, WID)
        for a in (forget_lane_anchor, present_boost, lane_normal_scale, lane_normal_shift)
    ]
    sds = jax.ShapeDtypeStruct
    shapes = (
        sds((TAIL, WID), BF16),
        sds((2 * DRAFT, WID), BF16),
        sds((1024, 128), F32),
        sds((16, 128), BF16),
    )
    vm = pltpu.VMEM
    row, ints, drafts = vm((1, WID), F32), vm((1, 128), jnp.int32), vm((2 * DRAFT, WID), BF16)
    side, tile16, tile8 = vm((TAIL, SIDE), BF16), vm((REP, 16, 128), BF16), vm((REP, 8, 128), BF16)
    outs = pl.pallas_call(
        mix_kernel,
        name="time_mix",
        out_shape=shapes,
        in_specs=[ANY] * 20,
        out_specs=(VM,) * 4,
        scratch_shapes=[
            vm((TAIL, WID), BF16), drafts, vm((1024, 128), F32), vm((16, 128), BF16), row, row,
            ints, ints, ints, drafts, drafts, vm((RANK, WID), BF16), row, row, row, row,
            vm((TP * WID, WID), BF16), vm((WID, RANK), BF16), side, side,
            vm((128, 128), F32), vm((1024, 128), F32), tile16, tile16, tile8, tile8,
            vm((TAIL, WID), BF16), vm((TAIL, RANK), BF16), vm((HALF, WID), BF16), vm((HALF, RANK), BF16),
            vm((16, WID), BF16), vm((16, RANK), BF16), vm((16, WID), BF16), vm((16, RANK), BF16),
            vm((TP, ROWS, WID), BF16), vm((TP, ROWS, RANK), BF16), vm((ROWS, WID), F32),
            vm((HALF, WID), BF16), vm((HALF, RANK), BF16), vm((LATE, WID), BF16), vm((LATE, RANK), BF16),
            side, vm((TAIL, RANK), BF16), side, side,
            vm((PAIRS, 64, 128), BF16), vm((SPLIT, 64, 128), BF16),
            vm((STEPS * SPLIT, 2 * CHUNK, CHUNK), BF16), side, vm((TAIL, SIDE), F32),
            vm((STEPS * SPLIT, 128, CHUNK), BF16), vm((STEPS * SPLIT, 128, 128), F32),
            vm((SPLIT, 128, 128), F32), vm((SPLIT, 128, 128), F32), vm((TAIL, SIDE), F32), side, side,
            vm((2, 128, 128), F32), drafts, vm((2, PAIRS, 128, 128), F32), vm((3, PAIRS, 128, 128), F32),
            tile16, tile16, tile8, tile8, vm((16, RANK), BF16),
            DMA((19,)), DMA((TP,)), DMA, DMA, DMA, DMA, DMA, DMA, DMA, DMA, DMA((15,)), DMA((15,)),
            DMA((8,)), DMA((8,)), DMA((8,)), DMA((8,)), DMA((8,)), DMA((8,)),
            pltpu.SemaphoreType.REGULAR, pltpu.SemaphoreType.REGULAR,
        ],
        compiler_params=pltpu.CompilerParams(
            collective_id=0, has_side_effects=True, vmem_limit_bytes=56 << 20
        ),
    )(
        suffix_source.reshape(TAIL, WID),
        guess_lane_source.reshape(2 * DRAFT, WID),
        kernel_memory_saved.reshape(1024, 128),
        prior_source_saved.reshape(128, 16).T,
        content_blend_share.reshape(1, WID),
        forget_blend_share.reshape(1, WID),
        *small,
        guess_lane_accept.reshape(2 * DRAFT, WID),
        guess_lane_address.reshape(2 * DRAFT, WID),
        forget_expand_map,
        *chan,
        content_map,
        forget_shrink_map,
        suffix_accept.reshape(TAIL, WID),
        suffix_address.reshape(TAIL, WID),
    )
    tail, draft, state, prior = pl.pallas_call(
        place_kernel,
        name="place",
        out_shape=shapes,
        in_specs=[VM] * 4,
        out_specs=(ANY,) * 4,
        scratch_shapes=[DMA((4,))],
    )(*outs)
    return (
        tail.reshape(1, TAIL, WID),
        draft.reshape(2, DRAFT, WID),
        state.reshape(128, 1, WID),
        prior.T.reshape(128, 1, 16),
    )


def solution(mesh):
    rows, cols, chan = P("rep", None, "tp"), P(None, "tp"), P("tp")
    cache = P(None, "rep", "tp")
    return jax.shard_map(
        local,
        mesh=mesh,
        in_specs=(rows,) * 6 + (cols, P(), cols) + (chan,) * 6 + (cache, cache, P(), P(), P()),
        out_specs=(rows, rows, cache, cache),
        check_vma=False,
    )
```

```python
import jax
import jax.numpy as jnp
from jax import lax
from jax.experimental import pallas as pl
from jax.experimental.pallas import tpu as pltpu
from jax.sharding import PartitionSpec as P

SPAN = 64
DRAFT = 16
EPS = 0.00064
REP = 64
ROW = 8
TP = 4
WID = 1024
TAIL = 384
HALF = 192
LATE = 48
ROWS = HALF + 32
PIECE = 48
CHUNK = 32
PAIRS = 8
RANK = 128
F32 = jnp.float32
BF16 = jnp.bfloat16
MESH = pl.DeviceIdType.MESH

SIDE = WID // 2
SPLIT = PAIRS // 2
STEPS = TAIL // CHUNK

ITEMS = (
    ("p", 0, 192),
    ("x", 16, 32),
    ("x", 48, 48),
    ("x", 96, 48),
    ("x", 144, 48),
    ("x", 0, 16),
    ("x", 192, 32),
    ("p", 192, 48),
)
RELAY_RIGHT = (1, 3, 5)
DIRECT = (0, 7)


def iota(shape, dim):
    return lax.broadcasted_iota(jnp.int32, shape, dim)


def nt(a, b):
    return lax.dot_general(a, b, (((1,), (1,)), ((), ())), preferred_element_type=F32)


def tn(a, b):
    return lax.dot_general(a, b, (((0,), (0,)), ((), ())), preferred_element_type=F32)


def mm(a, b):
    return jnp.dot(a, b, preferred_element_type=F32)


def owner_tables(own_ref, spans_ref, adm_ref, perm_ref):
    hot = (iota((128, 128), 0) == own_ref[...]).astype(F32)
    row = iota((8, 128), 0)
    long_q = (spans_ref[...] > DRAFT).astype(F32)
    facts = jnp.where(row == 0, long_q, jnp.where(row == 1, adm_ref[...].astype(F32), 0.0))
    by_slot = mm(facts.astype(BF16), hot.astype(BF16))
    perm_ref[...] = hot.T
    dealt = jnp.concatenate([perm_ref[pl.ds(0, 64, stride=2), :], perm_ref[pl.ds(1, 64, stride=2), :]], axis=0)
    return dealt, by_slot


def fact(by_slot, row, slot):
    pick = iota((8, 128), 1) == slot
    here = jnp.where(pick & (iota((8, 128), 0) == row), by_slot, 0.0)
    return jnp.sum(jnp.sum(here, axis=1, keepdims=True), axis=0, keepdims=True)


def greet_near(barrier, g, t):
    near = [(g, lax.rem(t + d, TP)) for d in range(1, TP)]
    near += [(g - lax.rem(g, ROW) + lax.rem(g + d, ROW), t) for d in range(1, ROW)]
    near += [(lax.rem(g + ROW * d, REP), t) for d in (1, 2, 6, 7)]
    for to in near:
        pl.semaphore_signal(barrier, inc=1, device_id=to, device_id_type=MESH)
    return len(near)


def pass_on(sem, g, t, steps):
    for d in steps:
        pl.semaphore_signal(sem, inc=1, device_id=(lax.rem(g + ROW * d, REP), t), device_id_type=MESH)


def scatter_rep(src, dst, send, recv, g, t):
    def one(d, _):
        to = lax.rem(g + d, REP)
        pltpu.make_async_remote_copy(
            src_ref=src.at[to],
            dst_ref=dst.at[g],
            send_sem=send,
            recv_sem=recv,
            device_id=(to, t),
            device_id_type=MESH,
        ).start()
        return 0

    lax.fori_loop(1, REP, one, 0, unroll=7)


def wait_rep(buf, sem):
    part = buf.at[pl.ds(0, REP - 1)]
    pltpu.make_async_copy(part, part, sem).wait()


def mixed(x, prev, share):
    return x + (prev - x) * share


def halves(a):
    low = iota(a.shape, 1) < SPAN
    zero = jnp.zeros_like(a)
    return jnp.concatenate([jnp.where(low, a, zero), jnp.where(low, zero, a)], axis=0)


def lanes(p):
    return slice(128 * p, 128 * p + 128)


def stack(a, pairs):
    return jnp.concatenate([a[:, lanes(p)] for p in range(pairs)], axis=0)


def running(log, n):
    tri = (iota((n, n), 0) >= iota((n, n), 1)).astype(BF16)
    hi = log.astype(BF16)
    lo = (log - hi.astype(F32)).astype(BF16)
    return mm(tri, hi) + mm(tri, lo)


def column(row):
    hi = row.astype(BF16).astype(F32)
    rest = row - hi
    mid = rest.astype(BF16).astype(F32)
    low = rest - mid
    at = iota((16, 128), 0)
    parts = jnp.where(at == 0, hi, jnp.where(at == 1, mid, jnp.where(at == 2, low, 0.0)))
    return tn(parts.astype(BF16), jnp.ones((16, 128), BF16))


def scaled(r, k, incl, log, n):
    excl = incl - log
    mid = incl[n // 2 : n // 2 + 1]
    q = (r * jnp.exp(jnp.minimum(excl - mid, 80.0))).astype(BF16)
    kk = (k * jnp.exp(jnp.minimum(mid - incl, 80.0))).astype(BF16)
    return q, kk, (r * jnp.exp(excl)).astype(BF16)


def scored(q, kk, n):
    strict = iota((2 * n, n), 0) % n > iota((2 * n, n), 1)
    return jnp.where(strict, nt(halves(q), kk), 0.0).astype(BF16)


def normed(y, heads_sum, scale, shift, n, pairs):
    hi = y.astype(BF16)
    lo = (y - hi.astype(F32)).astype(BF16)
    center = y - (mm(hi, heads_sum) + mm(lo, heads_sum)) * (1.0 / SPAN)
    spread = mm((center * center).astype(BF16), heads_sum) * (1.0 / SPAN)
    o = center * lax.rsqrt(spread + EPS)
    return jnp.concatenate(
        [o[n * p : n * p + n] * scale[:, lanes(p)] + shift[:, lanes(p)] for p in range(pairs)], axis=1
    )


def mix_kernel(
    x_hbm, gx_hbm, km_hbm, p0_hbm, mc_hbm, mf_hbm, own_hbm, spans_hbm, adm_hbm, gr_hbm, gk_hbm, ex_hbm,
    anchor_hbm, boost_hbm, scale_hbm, shift_hbm, w_hbm, sh_hbm, rt_hbm, kt_hbm,
    tail_hbm, draft_hbm, rgot, prior_hbm, req_hbm,
    x_ref, gx_ref, km_ref, p0_ref, mc_ref, mf_ref, own_ref, spans_ref, adm_ref, gr_ref, gk_ref, ex_ref,
    anchor_ref, boost_ref, scale_ref, shift_ref, w_ref, sh_ref, rown, kown,
    perm_ref, wide_ref, sbuf, sgot, pbuf, pgot, xv_ref, part_ref, xin, pin, zsend, zpart, zin, zpin,
    xg, pg, acc, vh, lh, vl_ref, ll_ref, vt_ref, lt_ref, rmate, kmate, st0_ref, stm_ref,
    sc_ref, ri_ref, gain_ref, kd_ref, keep_ref, st_ref, endm_ref, y_ref, o_ref, om_ref,
    dy_ref, dri_ref, du_ref, dk_ref, rbuf, ebuf, egot, lz_ref,
    dkd_ref, dsc_ref, tail_ref, draft_ref, prior_ref, req_ref, out_sem,
    in_sem, w_sem, st_send, st_recv, p_send, p_recv, e_send, e_recv, b_send, b_recv, mate_send, mate_recv,
    right_send, left_recv, left_send, right_recv, hop_send, hop_recv, round1, round2,
):
    g, t = lax.axis_index("rep"), lax.axis_index("tp")
    core = lax.rem(g, 2)
    mate = g + 1 - 2 * core
    right, left, far = lax.rem(t + 1, TP), lax.rem(t + 3, TP), lax.rem(t + 2, TP)
    mine = pl.multiple_of(core * HALF, 16)
    other = pl.multiple_of((1 - core) * HALF, 16)
    cols = pl.ds(pl.multiple_of(core * SIDE, 128), SIDE)
    mate_cols = pl.ds(pl.multiple_of((1 - core) * SIDE, 128), SIDE)

    own_rows = pl.ds(pl.multiple_of(t * WID, WID), WID)
    plain = (
        (x_hbm, x_ref), (mf_hbm, mf_ref), (mc_hbm, mc_ref), (sh_hbm.at[own_rows], sh_ref), (own_hbm, own_ref),
        (spans_hbm, spans_ref), (adm_hbm, adm_ref), (p0_hbm, p0_ref), (gx_hbm, gx_ref), (km_hbm, km_ref),
        (rt_hbm.at[:, cols], rown), (kt_hbm.at[:, cols], kown), (gr_hbm, gr_ref), (gk_hbm, gk_ref), (ex_hbm, ex_ref),
        (anchor_hbm, anchor_ref), (boost_hbm, boost_ref), (scale_hbm, scale_ref), (shift_hbm, shift_ref),
    )

    def in_copy(i):
        return pltpu.make_async_copy(plain[i][0], plain[i][1], in_sem.at[i])

    def w_copy(k):
        rows = pl.ds(k * WID, WID)
        return pltpu.make_async_copy(w_hbm.at[rows], w_ref.at[rows], w_sem.at[k])

    for i in range(len(plain)):
        in_copy(i).start()
    for k in range(TP):
        w_copy(k).start()

    barrier = pltpu.get_barrier_semaphore()
    greeted = greet_near(barrier, g, t)

    for i in range(4):
        in_copy(i).wait()
    mc, mf = mc_ref[...], mf_ref[...]

    def mix_rows(j, _):
        r0 = pl.multiple_of(j * PIECE, 16)
        x = x_ref[pl.ds(r0, PIECE), :].astype(F32)
        ahead = x_ref[pl.ds(pl.multiple_of(jnp.maximum(r0 - 16, 0), 16), 16), :].astype(F32)
        prev = jnp.where(iota((PIECE, WID), 0) == 0, ahead[15:16], pltpu.roll(x, 1, 0))
        xv_ref[pl.ds(r0, PIECE), :] = mixed(x, prev, mc).astype(BF16)
        part_ref[pl.ds(r0, PIECE), :] = mm(mixed(x, prev, mf).astype(BF16), sh_ref[...]).astype(BF16)
        return 0

    lax.fori_loop(0, TAIL // PIECE, mix_rows, 0)
    for i in range(4, len(plain)):
        in_copy(i).wait()
    pl.semaphore_wait(barrier, greeted)
    pass_on(round1, g, t, (1, 2, 6, 7))

    moves = {
        0: (part_ref.at[pl.ds(other, HALF)], pin),
        5: (rt_hbm.at[:, mate_cols], rmate),
        6: (kt_hbm.at[:, mate_cols], kmate),
        7: (zsend, zin),
        8: (zpart, zpin),
        9: (lh, lt_ref.at[pl.ds(mine, HALF)]),
        10: (vh.at[:, mate_cols], vt_ref.at[pl.ds(mine, HALF)]),
        11: (st0_ref.at[pl.ds((1 - core) * SPLIT, SPLIT)], stm_ref),
        12: (st_ref, endm_ref),
        13: (o_ref, om_ref),
        14: (ll_ref.at[pl.ds(32, 16)], lz_ref),
    }
    for j in range(4):
        moves[1 + j] = (xv_ref.at[pl.ds(other + j * PIECE, PIECE)], xin.at[pl.ds(j * PIECE, PIECE)])

    def to_mate(j):
        return pltpu.make_async_remote_copy(
            src_ref=moves[j][0],
            dst_ref=moves[j][1],
            send_sem=mate_send.at[j],
            recv_sem=mate_recv.at[j],
            device_id=(mate, t),
            device_id_type=MESH,
        )

    def part_of(item, source):
        kind, r0, n = ITEMS[item]
        return (xg if kind == "x" else pg).at[source, pl.ds(r0, n)]

    def move(item, source, to, send, recv):
        return pltpu.make_async_remote_copy(
            src_ref=part_of(item, source),
            dst_ref=part_of(item, source),
            send_sem=send.at[item],
            recv_sem=recv.at[item],
            device_id=(g, to),
            device_id_type=MESH,
        )

    def give(item):
        move(item, t, right, right_send, left_recv).start()
        move(item, t, left, left_send, right_recv).start()
        if item in DIRECT:
            move(item, t, far, hop_send, hop_recv).start()

    def hand_on(item):
        move(item, left, right, right_send, left_recv).wait_recv()
        if item in RELAY_RIGHT:
            move(item, left, right, hop_send, hop_recv).start()
        move(item, right, left, left_send, right_recv).wait_recv()
        if item not in RELAY_RIGHT + DIRECT:
            move(item, right, left, hop_send, hop_recv).start()

    def far_item(item):
        move(item, far, right, hop_send, hop_recv).wait_recv()

    for j in range(5):
        to_mate(j).start()

    dealt, by_slot = owner_tables(own_ref, spans_ref, adm_ref, perm_ref)
    by_req = dealt.T.astype(BF16)
    dealt = dealt.astype(BF16)
    long_own = fact(by_slot, 0, 2 * g) > 0.5
    sent = nt(dealt, p0_ref[...])
    wide_ref[...] = jnp.zeros_like(wide_ref)
    wide_ref[pl.ds(0, 64, stride=8), 0:16] = sent[0:64]
    wide_ref[pl.ds(1, 64, stride=8), 0:16] = sent[64:128]
    pbuf[...] = wide_ref[0:512, :].astype(BF16).reshape(64, 8, 128)
    pgot[g] = pbuf[g]

    to_mate(0).wait_recv()
    pg[t, 0:HALF, :] = jnp.where(long_own, part_ref[pl.ds(mine, HALF), :], pin[...])
    give(0)
    for j in range(4):
        to_mate(1 + j).wait_recv()
        rows = pl.ds(j * PIECE, PIECE)
        xg[t, rows, :] = jnp.where(long_own, xv_ref[pl.ds(mine + j * PIECE, PIECE), :], xin[rows, :])
        give(1 + j)
    to_mate(5).start()
    to_mate(6).start()
    pl.semaphore_wait(round1, 4)
    pass_on(round2, g, t, (3, 4, 5))

    hand_on(0)
    far_item(0)

    def low_rank(r0, n):
        parts = [pg[k, r0 : r0 + n, :].astype(F32) for k in range(TP)]
        return jnp.tanh(parts[0] + parts[1] + parts[2] + parts[3]).astype(BF16)

    lh[...] = low_rank(0, HALF)
    to_mate(9).start()
    lt_ref[pl.ds(mine, HALF), :] = lh[...]
    pl.semaphore_wait(round2, 3)
    scatter_rep(pbuf, pgot, p_send, p_recv, g, t)
    hand_on(1)

    for c in range(8):
        rows = mm(dealt, km_ref[pl.ds(c, 128, stride=8), :].astype(BF16))
        wide_ref[pl.ds(c, 64, stride=16), :] = rows[0:64]
        wide_ref[pl.ds(8 + c, 64, stride=16), :] = rows[64:128]
    sbuf[...] = wide_ref[...].astype(BF16).reshape(64, 16, 128)
    sgot[g] = sbuf[g]
    scatter_rep(sbuf, sgot, st_send, st_recv, g, t)
    hand_on(2)

    same = iota((128, 128), 0) // SPAN == iota((128, 128), 1) // SPAN
    heads_sum = same.astype(BF16)
    anchor, boost, scale, shift = anchor_ref[...], boost_ref[...], scale_ref[...], shift_ref[...]

    def ready(i, _):
        rows = pl.ds(pl.multiple_of(i * CHUNK, 16), CHUNK)
        log = -jnp.exp(anchor_ref[:, cols] + mm(lt_ref[rows, :], ex_ref[:, cols]))
        r = jnp.where(long_own, rown[rows, :], rmate[rows, :]).astype(F32)
        k = jnp.where(long_own, kown[rows, :], kmate[rows, :]).astype(F32)
        incl = running(log, CHUNK)
        q, kk, ri = scaled(r, k, incl, log, CHUNK)
        ri_ref[rows, :] = ri
        last = incl[CHUNK - 1 : CHUNK]
        kd = k * jnp.exp(last - incl)
        keep = jnp.exp(last)
        gain = mm(stack((r * boost_ref[:, cols] * k).astype(BF16), SPLIT), heads_sum)
        for p in range(SPLIT):
            c = lanes(p)
            gain_ref[rows, c] = gain[CHUNK * p : CHUNK * p + CHUNK]
            sc_ref[SPLIT * i + p] = scored(q[:, c], kk[:, c], CHUNK)
            kd_ref[SPLIT * i + p] = kd[:, c].T.astype(BF16)
            keep_ref[SPLIT * i + p] = column(keep[:, c])
        return 0

    def product(source, add):
        def tile(n, _):
            c = pl.ds(pl.multiple_of(n * 256, 256), 256)
            out = mm(xg[source], w_ref[pl.ds(pl.multiple_of(source * WID, WID), WID), c])
            acc[:, c] = acc[:, c] + out if add else out
            return 0

        lax.fori_loop(0, WID // 256, tile, 0, unroll=2)

    to_mate(5).wait_recv()
    to_mate(6).wait_recv()
    to_mate(9).wait_recv()

    spread = (iota((128, WID), 1) // SPAN == iota((128, WID), 0)).astype(BF16)
    own_lane = iota((64, WID), 1) % SPAN == iota((64, WID), 0)
    row16 = iota((16, WID), 0)
    firsts = []

    def late_rows():
        wait_rep(pgot, p_recv)
        wide_ref[0:512, :] = pgot[...].reshape(512, 128).astype(F32)
        before = []
        for s in range(2):
            vals = mm(wide_ref[pl.ds(s, 64, stride=8), :].astype(BF16), spread)
            before.append(jnp.sum(jnp.where(own_lane, vals, 0.0), axis=0, keepdims=True))
        final = x_ref[TAIL - 16 : TAIL, :].astype(F32)[15:16]
        firsts.extend([jnp.where(long_own, final, before[0]), before[1]])
        cur = [x_ref[0:16, :].astype(F32), gx_ref[0:16, :].astype(F32), gx_ref[16:32, :].astype(F32)]
        ahead = [jnp.where(row16 == 0, f, pltpu.roll(x, 1, 0)) for x, f in zip(cur, before[:1] + firsts)]
        zsend[...] = mixed(cur[0], ahead[0], mc).astype(BF16)
        zpart[...] = mm(mixed(cur[0], ahead[0], mf).astype(BF16), sh_ref[...]).astype(BF16)
        to_mate(7).start()
        to_mate(8).start()
        for s in range(2):
            at = HALF + 16 * s
            xg[t, at : at + 16, :] = mixed(cur[1 + s], ahead[1 + s], mc).astype(BF16)
            pg[t, at : at + 16, :] = mm(mixed(cur[1 + s], ahead[1 + s], mf).astype(BF16), sh_ref[...]).astype(BF16)

    def give_late():
        to_mate(7).wait_recv()
        to_mate(8).wait_recv()
        at = HALF + 32
        pg[t, at : at + 16, :] = jnp.where(long_own, zpart[...], zpin[...])
        first_rows = jnp.where(long_own, zsend[...], zin[...])
        xg[t, 0:16, :] = jnp.where(core == 0, first_rows, xg[t, 0:16, :])
        for item in (7, 5, 6):
            give(item)

    counts = []

    def edges_out():
        wide_ref[0:512, :] = jnp.zeros((512, 128), F32)
        for s in range(2):
            count = fact(by_slot, 1, 2 * g + s).astype(jnp.int32)
            counts.append(count)
            rows = gx_ref[DRAFT * s : DRAFT * s + DRAFT, :].astype(F32)
            edge = jnp.sum(jnp.where(row16 == count - 1, rows, 0.0), axis=0, keepdims=True)
            edge = jnp.where(count > 0, edge, firsts[s])
            wide_ref[pl.ds(s, 64, stride=8), :] = nt(jnp.where(own_lane, edge, 0.0).astype(BF16), spread)
        ebuf[...] = wide_ref[0:512, :].astype(BF16).reshape(64, 8, 128)
        egot[g] = ebuf[g]
        scatter_rep(ebuf, egot, e_send, e_recv, g, t)

    def draft_ready(s):
        rows = slice(DRAFT * s, DRAFT * s + DRAFT)
        log = -jnp.exp(anchor + mm(ll_ref[rows, :], ex_ref[...]))
        r, k = gr_ref[rows, :].astype(F32), gk_ref[rows, :].astype(F32)
        incl = running(log, DRAFT)
        q, kk, ri = scaled(r, k, incl, log, DRAFT)
        dri_ref[rows, :] = ri
        gain = mm(stack((r * boost * k).astype(BF16), PAIRS), heads_sum)
        taken = row16 < counts[s]
        upto = jnp.sum(jnp.where(taken, log, 0.0), axis=0, keepdims=True)
        weight = jnp.where(taken, jnp.exp(jnp.where(taken, upto - incl, 0.0)), 0.0)
        dkd_ref[rows, :] = (k * weight).astype(BF16)
        keep = jnp.exp(upto)
        dy_ref[s] = gain
        for p in range(PAIRS):
            c = lanes(p)
            dsc_ref[PAIRS * s + p] = scored(q[:, c], kk[:, c], DRAFT)
            dk_ref[s, p] = column(keep[:, c])

    def draft_values(s):
        rows = slice(DRAFT * s, DRAFT * s + DRAFT)
        low16 = iota((DRAFT, 128), 1) < SPAN
        for p in range(PAIRS):
            c = lanes(p)
            at = slice(DRAFT * p, DRAFT * p + DRAFT)
            v = vl_ref[rows, c]
            both = mm(dsc_ref[PAIRS * s + p], v)
            inner = jnp.where(low16, both[0:DRAFT], both[DRAFT : 2 * DRAFT])
            dy_ref[s, at, :] = inner + dy_ref[s, at, :] * v.astype(F32)
            du_ref[s, p] = jnp.where(same, tn(dkd_ref[rows, c], v), 0.0)

    lax.fori_loop(1, 4, ready, 0, unroll=3)
    hand_on(3)
    late_rows()
    lax.fori_loop(4, 6, ready, 0, unroll=2)
    give_late()
    hand_on(4)
    lax.fori_loop(6, 9, ready, 0, unroll=3)
    edges_out()
    for k in range(TP):
        w_copy(k).wait()
    product(t, False)
    hand_on(7)
    hand_on(5)
    hand_on(6)
    far_item(7)
    ll_ref[...] = low_rank(HALF, LATE)
    to_mate(14).start()
    product(left, True)
    wait_rep(sgot, st_recv)
    wide_ref[...] = sgot[...].reshape(1024, 128).astype(F32)
    for p in range(PAIRS):
        st0_ref[p] = wide_ref[pl.ds(p, 64, stride=16), :].astype(BF16)
    to_mate(11).start()
    for p in range(PAIRS):
        dk_ref[2, p] = halves(wide_ref[pl.ds(8 + p, 64, stride=16), :])
    lax.fori_loop(9, STEPS, ready, 0, unroll=3)
    to_mate(14).wait_recv()
    head = jnp.where(core == 0, ll_ref[32:33, :], lz_ref[0:1, :])
    lt_ref[0:16, :] = jnp.where(iota((16, RANK), 0) == 0, head, lt_ref[0:16, :])
    ready(0, 0)
    product(right, True)
    to_mate(11).wait_recv()
    for p in range(SPLIT):
        start = jnp.where(long_own, st0_ref[core * SPLIT + p], stm_ref[p])
        st_ref[p] = halves(start.astype(F32))
    for s in range(2):
        draft_ready(s)
    for item in range(1, 7):
        far_item(item)
    product(far, True)
    vh[...] = acc[0:HALF, :].astype(BF16)
    to_mate(10).start()
    vl_ref[...] = acc[HALF:ROWS, :].astype(BF16)
    vt_ref[pl.ds(mine, HALF), :] = vh[:, cols]

    def accept(s, p, state):
        rows = slice(DRAFT * s, DRAFT * s + DRAFT)
        at = slice(DRAFT * p, DRAFT * p + DRAFT)
        dy_ref[s, at, :] = dy_ref[s, at, :] + mm(dri_ref[rows, lanes(p)], state.astype(BF16))
        end = state * dk_ref[s, p] + du_ref[s, p]
        wide_ref[pl.ds(512 * s + p, 64, stride=8), :] = end[0:64] + end[64:128]

    def give_back(s):
        rbuf[s] = wide_ref[512 * s : 512 * s + 512, :].astype(BF16).reshape(64, 8, 128)
        rgot[s, g] = rbuf[s, g]
        scatter_rep(rbuf.at[s], rgot.at[s], b_send.at[s], b_recv.at[s], g, t)

    draft_values(1)
    for p in range(PAIRS):
        accept(1, p, dk_ref[2, p])
    give_back(1)

    to_mate(10).wait_recv()
    low32 = iota((CHUNK, 128), 1) < SPAN

    def step(i, _):
        rows = pl.ds(pl.multiple_of(i * CHUNK, 16), CHUNK)
        for p in range(SPLIT):
            c = lanes(p)
            v = vt_ref[rows, c]
            both = mm(sc_ref[SPLIT * i + p], v)
            state = st_ref[p]
            y = jnp.where(low32, both[0:CHUNK], both[CHUNK : 2 * CHUNK])
            y_ref[rows, c] = y + mm(ri_ref[rows, c], state.astype(BF16)) + gain_ref[rows, c] * v.astype(F32)
            st_ref[p] = state * keep_ref[SPLIT * i + p] + jnp.where(same, mm(kd_ref[SPLIT * i + p], v), 0.0)
        return 0

    lax.fori_loop(0, STEPS, step, 0, unroll=6)
    to_mate(12).start()

    draft_values(0)

    def finish(i, _):
        rows = pl.ds(pl.multiple_of(i * CHUNK, 16), CHUNK)
        y = stack(y_ref[rows, :], SPLIT)
        o_ref[rows, :] = normed(y, heads_sum, scale_ref[:, cols], shift_ref[:, cols], CHUNK, SPLIT).astype(BF16)
        return 0

    lax.fori_loop(0, STEPS // 2, finish, 0, unroll=2)
    to_mate(12).wait_recv()
    for p in range(PAIRS):
        end = jnp.where(core == p // SPLIT, st_ref[p % SPLIT], endm_ref[p % SPLIT])
        accept(0, p, jnp.where(long_own, end, halves(st0_ref[p].astype(F32))))
    give_back(0)
    lax.fori_loop(STEPS // 2, STEPS, finish, 0, unroll=2)
    to_mate(13).start()
    for s in range(2):
        draft_ref[DRAFT * s : DRAFT * s + DRAFT, :] = normed(
            dy_ref[s], heads_sum, scale, shift, DRAFT, PAIRS
        ).astype(BF16)
    tail_ref[:, cols] = jnp.where(long_own, o_ref[...], jnp.zeros((TAIL, SIDE), BF16))

    wait_rep(egot, e_recv)
    wide_ref[0:512, :] = egot[...].reshape(512, 128).astype(F32)
    edges = jnp.concatenate([wide_ref[pl.ds(0, 64, stride=8), :], wide_ref[pl.ds(1, 64, stride=8), :]], axis=0)
    prior_ref[...] = tn(edges.astype(BF16), dealt)[0:16].astype(BF16)
    to_mate(13).wait_recv()
    tail_ref[:, mate_cols] = jnp.where(long_own, om_ref[...], jnp.zeros((TAIL, SIDE), BF16))
    req_ref[...] = by_req
    outs = ((tail_ref, tail_hbm), (draft_ref, draft_hbm), (prior_ref, prior_hbm), (req_ref, req_hbm))
    puts = [pltpu.make_async_copy(a, b, out_sem.at[i]) for i, (a, b) in enumerate(outs)]
    for put in puts:
        put.start()
    for s in range(2):
        wait_rep(rgot.at[s], b_recv.at[s])
    for put in puts:
        put.wait()

    wait_rep(pbuf, p_send)
    wait_rep(sbuf, st_send)
    wait_rep(ebuf, e_send)
    for s in range(2):
        wait_rep(rbuf.at[s], b_send.at[s])
    for j in range(15):
        to_mate(j).wait_send()
    for item in range(8):
        move(item, t, right, right_send, left_recv).wait_send()
        move(item, t, left, left_send, right_recv).wait_send()
        move(item, far, right, hop_send, hop_recv).wait_send()


def place_kernel(
    tail_in, draft_in, back_in, prior_in, req_in, tail_out, draft_out, state_out, prior_out,
    tail, draft, back, prior, req, wide, state, get_sem, put_sem,
):
    src, mid = (back_in, req_in, tail_in, draft_in, prior_in), (back, req, tail, draft, prior)
    gets = [pltpu.make_async_copy(a, b, get_sem.at[i]) for i, (a, b) in enumerate(zip(src, mid))]
    outs = ((tail, tail_out), (draft, draft_out), (prior, prior_out), (state, state_out))
    puts = [pltpu.make_async_copy(a, b, put_sem.at[i]) for i, (a, b) in enumerate(outs)]
    for get in gets:
        get.start()
    gets[0].wait()
    gets[1].wait()
    wide[...] = back[...].reshape(1024, 128).astype(F32)
    for i in range(3):
        gets[2 + i].wait()
        puts[i].start()
    for c in range(8):
        rows = jnp.concatenate(
            [wide[pl.ds(c, 64, stride=8), :], wide[pl.ds(512 + c, 64, stride=8), :]], axis=0
        )
        state[pl.ds(c, 128, stride=8), :] = mm(req[...], rows.astype(BF16))
    puts[3].start()
    for put in puts:
        put.wait()


VM = pl.BlockSpec(memory_space=pltpu.VMEM)
ANY = pl.BlockSpec(memory_space=pl.ANY)
DMA = pltpu.SemaphoreType.DMA


def local(
    suffix_source, suffix_accept, suffix_address, guess_lane_source, guess_lane_accept, guess_lane_address,
    content_map, forget_shrink_map, forget_expand_map, forget_lane_anchor, present_boost,
    content_blend_share, forget_blend_share, lane_normal_scale, lane_normal_shift,
    kernel_memory_saved, prior_source_saved, lane_owner, request_spans, admitted_guesses,
):
    small = [a.reshape(1, 128) for a in (lane_owner, request_spans, admitted_guesses)]
    chan = [
        a.reshape(1, WID)
        for a in (forget_lane_anchor, present_boost, lane_normal_scale, lane_normal_shift)
    ]
    sds = jax.ShapeDtypeStruct
    shapes = (
        sds((TAIL, WID), BF16),
        sds((2 * DRAFT, WID), BF16),
        sds((1024, 128), F32),
        sds((16, 128), BF16),
    )
    vm = pltpu.VMEM
    row, ints, drafts = vm((1, WID), F32), vm((1, 128), jnp.int32), vm((2 * DRAFT, WID), BF16)
    side, tile16, tile8 = vm((TAIL, SIDE), BF16), vm((REP, 16, 128), BF16), vm((REP, 8, 128), BF16)
    outs = pl.pallas_call(
        mix_kernel,
        name="time_mix",
        out_shape=(shapes[0], shapes[1], sds((2, REP, 8, 128), BF16), shapes[3], sds((128, 128), BF16)),
        in_specs=[ANY] * 20,
        out_specs=(ANY, ANY, VM, ANY, ANY),
        scratch_shapes=[
            vm((TAIL, WID), BF16), drafts, vm((1024, 128), F32), vm((16, 128), BF16), row, row,
            ints, ints, ints, drafts, drafts, vm((RANK, WID), BF16), row, row, row, row,
            vm((TP * WID, WID), BF16), vm((WID, RANK), BF16), side, side,
            vm((128, 128), F32), vm((1024, 128), F32), tile16, tile16, tile8, tile8,
            vm((TAIL, WID), BF16), vm((TAIL, RANK), BF16), vm((HALF, WID), BF16), vm((HALF, RANK), BF16),
            vm((16, WID), BF16), vm((16, RANK), BF16), vm((16, WID), BF16), vm((16, RANK), BF16),
            vm((TP, ROWS, WID), BF16), vm((TP, HALF + LATE, RANK), BF16), vm((ROWS, WID), F32),
            vm((HALF, WID), BF16), vm((HALF, RANK), BF16), vm((32, WID), BF16), vm((LATE, RANK), BF16),
            side, vm((TAIL, RANK), BF16), side, side,
            vm((PAIRS, 64, 128), BF16), vm((SPLIT, 64, 128), BF16),
            vm((STEPS * SPLIT, 2 * CHUNK, CHUNK), BF16), side, vm((TAIL, SIDE), F32),
            vm((STEPS * SPLIT, 128, CHUNK), BF16), vm((STEPS * SPLIT, 128, 128), F32),
            vm((SPLIT, 128, 128), F32), vm((SPLIT, 128, 128), F32), vm((TAIL, SIDE), F32), side, side,
            vm((2, 128, 128), F32), drafts, vm((2, PAIRS, 128, 128), F32), vm((3, PAIRS, 128, 128), F32),
            vm((2, REP, 8, 128), BF16), tile8, tile8, vm((16, RANK), BF16),
            drafts, vm((2 * PAIRS, 2 * DRAFT, DRAFT), BF16), vm((TAIL, WID), BF16), drafts, vm((16, 128), BF16),
            vm((128, 128), BF16), DMA((4,)),
            DMA((19,)), DMA((TP,)), DMA, DMA, DMA, DMA, DMA, DMA, DMA((2,)), DMA((2,)), DMA((15,)), DMA((15,)),
            DMA((8,)), DMA((8,)), DMA((8,)), DMA((8,)), DMA((8,)), DMA((8,)),
            pltpu.SemaphoreType.REGULAR, pltpu.SemaphoreType.REGULAR,
        ],
        compiler_params=pltpu.CompilerParams(
            collective_id=0, has_side_effects=True, vmem_limit_bytes=56 << 20
        ),
    )(
        suffix_source.reshape(TAIL, WID),
        guess_lane_source.reshape(2 * DRAFT, WID),
        kernel_memory_saved.reshape(1024, 128),
        prior_source_saved.reshape(128, 16).T,
        content_blend_share.reshape(1, WID),
        forget_blend_share.reshape(1, WID),
        *small,
        guess_lane_accept.reshape(2 * DRAFT, WID),
        guess_lane_address.reshape(2 * DRAFT, WID),
        forget_expand_map,
        *chan,
        content_map,
        forget_shrink_map,
        suffix_accept.reshape(TAIL, WID),
        suffix_address.reshape(TAIL, WID),
    )
    tail, draft, state, prior = pl.pallas_call(
        place_kernel,
        name="place",
        out_shape=shapes,
        in_specs=[ANY] * 5,
        out_specs=(ANY,) * 4,
        scratch_shapes=[
            vm((TAIL, WID), BF16), drafts, vm((2, REP, 8, 128), BF16), vm((16, 128), BF16),
            vm((128, 128), BF16), vm((1024, 128), F32), vm((1024, 128), F32), DMA((5,)), DMA((4,)),
        ],
    )(*outs)
    return (
        tail.reshape(1, TAIL, WID),
        draft.reshape(2, DRAFT, WID),
        state.reshape(128, 1, WID),
        prior.T.reshape(128, 1, 16),
    )


def solution(mesh):
    rows, cols, chan = P("rep", None, "tp"), P(None, "tp"), P("tp")
    cache = P(None, "rep", "tp")
    return jax.shard_map(
        local,
        mesh=mesh,
        in_specs=(rows,) * 6 + (cols, P(), cols) + (chan,) * 6 + (cache, cache, P(), P(), P()),
        out_specs=(rows, rows, cache, cache),
        check_vma=False,
    )
```

```python
import jax
import jax.numpy as jnp
from jax import lax
from jax.experimental import pallas as pl
from jax.experimental.pallas import tpu as pltpu
from jax.sharding import PartitionSpec as P

SPAN = 64
DRAFT = 16
EPS = 0.00064
REP = 64
ROW = 8
TP = 4
WID = 1024
TAIL = 384
HALF = 192
LATE = 48
ROWS = HALF + 32
PIECE = 48
CHUNK = 32
PAIRS = 8
RANK = 128
F32 = jnp.float32
BF16 = jnp.bfloat16
MESH = pl.DeviceIdType.MESH

SIDE = WID // 2
SPLIT = PAIRS // 2
STEPS = TAIL // CHUNK

ITEMS = (
    ("p", 0, 192),
    ("x", 16, 32),
    ("x", 48, 48),
    ("x", 96, 48),
    ("x", 144, 48),
    ("x", 0, 16),
    ("x", 192, 32),
    ("p", 192, 48),
)
RELAY_RIGHT = (1, 3, 5)
DIRECT = (0, 7)


def iota(shape, dim):
    return lax.broadcasted_iota(jnp.int32, shape, dim)


def nt(a, b):
    return lax.dot_general(a, b, (((1,), (1,)), ((), ())), preferred_element_type=F32)


def tn(a, b):
    return lax.dot_general(a, b, (((0,), (0,)), ((), ())), preferred_element_type=F32)


def mm(a, b):
    return jnp.dot(a, b, preferred_element_type=F32)


def owner_tables(own_ref, spans_ref, adm_ref, perm_ref):
    hot = (iota((128, 128), 0) == own_ref[...]).astype(F32)
    row = iota((8, 128), 0)
    long_q = (spans_ref[...] > DRAFT).astype(F32)
    facts = jnp.where(row == 0, long_q, jnp.where(row == 1, adm_ref[...].astype(F32), 0.0))
    by_slot = mm(facts.astype(BF16), hot.astype(BF16))
    perm_ref[...] = hot.T
    dealt = jnp.concatenate([perm_ref[pl.ds(0, 64, stride=2), :], perm_ref[pl.ds(1, 64, stride=2), :]], axis=0)
    return dealt, by_slot


def fact(by_slot, row, slot):
    pick = iota((8, 128), 1) == slot
    here = jnp.where(pick & (iota((8, 128), 0) == row), by_slot, 0.0)
    return jnp.sum(jnp.sum(here, axis=1, keepdims=True), axis=0, keepdims=True)


def greet_near(barrier, g, t):
    near = [(g, lax.rem(t + d, TP)) for d in range(1, TP)]
    near += [(g - lax.rem(g, ROW) + lax.rem(g + d, ROW), t) for d in range(1, ROW)]
    near += [(lax.rem(g + ROW * d, REP), t) for d in (1, 2, 6, 7)]
    for to in near:
        pl.semaphore_signal(barrier, inc=1, device_id=to, device_id_type=MESH)
    return len(near)


def pass_on(sem, g, t, steps):
    for d in steps:
        pl.semaphore_signal(sem, inc=1, device_id=(lax.rem(g + ROW * d, REP), t), device_id_type=MESH)


def scatter_rep(src, dst, send, recv, g, t):
    def one(d, _):
        to = lax.rem(g + d, REP)
        pltpu.make_async_remote_copy(
            src_ref=src.at[to],
            dst_ref=dst.at[g],
            send_sem=send,
            recv_sem=recv,
            device_id=(to, t),
            device_id_type=MESH,
        ).start()
        return 0

    lax.fori_loop(1, REP, one, 0, unroll=7)


def wait_rep(buf, sem):
    part = buf.at[pl.ds(0, REP - 1)]
    pltpu.make_async_copy(part, part, sem).wait()


def mixed(x, prev, share):
    return x + (prev - x) * share


def halves(a):
    low = iota(a.shape, 1) < SPAN
    zero = jnp.zeros_like(a)
    return jnp.concatenate([jnp.where(low, a, zero), jnp.where(low, zero, a)], axis=0)


def lanes(p):
    return slice(128 * p, 128 * p + 128)


def stack(a, pairs):
    return jnp.concatenate([a[:, lanes(p)] for p in range(pairs)], axis=0)


def running(log, n):
    tri = (iota((n, n), 0) >= iota((n, n), 1)).astype(BF16)
    hi = log.astype(BF16)
    lo = (log - hi.astype(F32)).astype(BF16)
    return mm(tri, hi) + mm(tri, lo)


def column(row):
    hi = row.astype(BF16).astype(F32)
    rest = row - hi
    mid = rest.astype(BF16).astype(F32)
    low = rest - mid
    at = iota((16, 128), 0)
    parts = jnp.where(at == 0, hi, jnp.where(at == 1, mid, jnp.where(at == 2, low, 0.0)))
    return tn(parts.astype(BF16), jnp.ones((16, 128), BF16))


def scaled(r, k, incl, log, n):
    excl = incl - log
    mid = incl[n // 2 : n // 2 + 1]
    q = (r * jnp.exp(jnp.minimum(excl - mid, 80.0))).astype(BF16)
    kk = (k * jnp.exp(jnp.minimum(mid - incl, 80.0))).astype(BF16)
    return q, kk, (r * jnp.exp(excl)).astype(BF16)


def scored(q, kk, n):
    strict = iota((2 * n, n), 0) % n > iota((2 * n, n), 1)
    return jnp.where(strict, nt(halves(q), kk), 0.0).astype(BF16)


def normed(y, heads_sum, scale, shift, n, pairs):
    hi = y.astype(BF16)
    lo = (y - hi.astype(F32)).astype(BF16)
    center = y - (mm(hi, heads_sum) + mm(lo, heads_sum)) * (1.0 / SPAN)
    spread = mm((center * center).astype(BF16), heads_sum) * (1.0 / SPAN)
    o = center * lax.rsqrt(spread + EPS)
    return jnp.concatenate(
        [o[n * p : n * p + n] * scale[:, lanes(p)] + shift[:, lanes(p)] for p in range(pairs)], axis=1
    )


def mix_kernel(
    x_hbm, gx_hbm, km_hbm, p0_hbm, mc_hbm, mf_hbm, own_hbm, spans_hbm, adm_hbm, gr_hbm, gk_hbm, ex_hbm,
    anchor_hbm, boost_hbm, scale_hbm, shift_hbm, w_hbm, sh_hbm, rt_hbm, kt_hbm,
    tail_hbm, draft_hbm, rgot, prior_hbm, req_hbm,
    x_ref, gx_ref, km_ref, p0_ref, mc_ref, mf_ref, own_ref, spans_ref, adm_ref, gr_ref, gk_ref, ex_ref,
    anchor_ref, boost_ref, scale_ref, shift_ref, w_ref, sh_ref, rown, kown,
    perm_ref, wide_ref, sbuf, sgot, pbuf, pgot, xv_ref, part_ref, xin, pin, zsend, zpart, zin, zpin,
    xg, pg, acc, vh, lh, vl_ref, ll_ref, vt_ref, lt_ref, rmate, kmate, st0_ref, stm_ref,
    sc_ref, ri_ref, gain_ref, kd_ref, keep_ref, st_ref, endm_ref, y_ref, o_ref, om_ref,
    dy_ref, dri_ref, du_ref, dk_ref, rbuf, ebuf, egot, lz_ref,
    dkd_ref, dsc_ref, tail_ref, draft_ref, prior_ref, req_ref, out_sem,
    in_sem, w_sem, st_send, st_recv, p_send, p_recv, e_send, e_recv, b_send, b_recv, mate_send, mate_recv,
    right_send, left_recv, left_send, right_recv, hop_send, hop_recv, round1, round2,
):
    g, t = lax.axis_index("rep"), lax.axis_index("tp")
    core = lax.rem(g, 2)
    mate = g + 1 - 2 * core
    right, left, far = lax.rem(t + 1, TP), lax.rem(t + 3, TP), lax.rem(t + 2, TP)
    mine = pl.multiple_of(core * HALF, 16)
    other = pl.multiple_of((1 - core) * HALF, 16)
    cols = pl.ds(pl.multiple_of(core * SIDE, 128), SIDE)
    mate_cols = pl.ds(pl.multiple_of((1 - core) * SIDE, 128), SIDE)

    own_rows = pl.ds(pl.multiple_of(t * WID, WID), WID)
    plain = (
        (x_hbm, x_ref), (mf_hbm, mf_ref), (mc_hbm, mc_ref), (sh_hbm.at[own_rows], sh_ref), (own_hbm, own_ref),
        (spans_hbm, spans_ref), (adm_hbm, adm_ref), (p0_hbm, p0_ref), (gx_hbm, gx_ref), (km_hbm, km_ref),
        (rt_hbm.at[:, cols], rown), (kt_hbm.at[:, cols], kown), (gr_hbm, gr_ref), (gk_hbm, gk_ref), (ex_hbm, ex_ref),
        (anchor_hbm, anchor_ref), (boost_hbm, boost_ref), (scale_hbm, scale_ref), (shift_hbm, shift_ref),
    )

    def in_copy(i):
        return pltpu.make_async_copy(plain[i][0], plain[i][1], in_sem.at[i])

    def w_copy(k):
        rows = pl.ds(k * WID, WID)
        return pltpu.make_async_copy(w_hbm.at[rows], w_ref.at[rows], w_sem.at[k])

    for i in range(len(plain)):
        in_copy(i).start()
    for k in range(TP):
        w_copy(k).start()

    barrier = pltpu.get_barrier_semaphore()
    greeted = greet_near(barrier, g, t)

    for i in range(4):
        in_copy(i).wait()
    mc, mf = mc_ref[...], mf_ref[...]

    def mix_rows(j, _):
        r0 = pl.multiple_of(j * PIECE, 16)
        x = x_ref[pl.ds(r0, PIECE), :].astype(F32)
        ahead = x_ref[pl.ds(pl.multiple_of(jnp.maximum(r0 - 16, 0), 16), 16), :].astype(F32)
        prev = jnp.where(iota((PIECE, WID), 0) == 0, ahead[15:16], pltpu.roll(x, 1, 0))
        xv_ref[pl.ds(r0, PIECE), :] = mixed(x, prev, mc).astype(BF16)
        part_ref[pl.ds(r0, PIECE), :] = mm(mixed(x, prev, mf).astype(BF16), sh_ref[...]).astype(BF16)
        return 0

    lax.fori_loop(0, TAIL // PIECE, mix_rows, 0)
    for i in range(4, len(plain)):
        in_copy(i).wait()
    pl.semaphore_wait(barrier, greeted)
    pass_on(round1, g, t, (1, 2, 6, 7))

    moves = {
        0: (part_ref.at[pl.ds(other, HALF)], pin),
        5: (rt_hbm.at[:, mate_cols], rmate),
        6: (kt_hbm.at[:, mate_cols], kmate),
        7: (zsend, zin),
        8: (zpart, zpin),
        9: (lh, lt_ref.at[pl.ds(mine, HALF)]),
        10: (vh.at[:, mate_cols], vt_ref.at[pl.ds(mine, HALF)]),
        11: (st0_ref.at[pl.ds((1 - core) * SPLIT, SPLIT)], stm_ref),
        12: (st_ref, endm_ref),
        13: (o_ref, om_ref),
        14: (ll_ref.at[pl.ds(32, 16)], lz_ref),
    }
    for j in range(4):
        moves[1 + j] = (xv_ref.at[pl.ds(other + j * PIECE, PIECE)], xin.at[pl.ds(j * PIECE, PIECE)])

    def to_mate(j):
        return pltpu.make_async_remote_copy(
            src_ref=moves[j][0],
            dst_ref=moves[j][1],
            send_sem=mate_send.at[j],
            recv_sem=mate_recv.at[j],
            device_id=(mate, t),
            device_id_type=MESH,
        )

    def part_of(item, source):
        kind, r0, n = ITEMS[item]
        return (xg if kind == "x" else pg).at[source, pl.ds(r0, n)]

    def move(item, source, to, send, recv):
        return pltpu.make_async_remote_copy(
            src_ref=part_of(item, source),
            dst_ref=part_of(item, source),
            send_sem=send.at[item],
            recv_sem=recv.at[item],
            device_id=(g, to),
            device_id_type=MESH,
        )

    def give(item):
        move(item, t, right, right_send, left_recv).start()
        move(item, t, left, left_send, right_recv).start()
        if item in DIRECT:
            move(item, t, far, hop_send, hop_recv).start()

    def hand_on(item):
        move(item, left, right, right_send, left_recv).wait_recv()
        if item in RELAY_RIGHT:
            move(item, left, right, hop_send, hop_recv).start()
        move(item, right, left, left_send, right_recv).wait_recv()
        if item not in RELAY_RIGHT + DIRECT:
            move(item, right, left, hop_send, hop_recv).start()

    def far_item(item):
        move(item, far, right, hop_send, hop_recv).wait_recv()

    for j in range(5):
        to_mate(j).start()

    dealt, by_slot = owner_tables(own_ref, spans_ref, adm_ref, perm_ref)
    by_req = dealt.T.astype(BF16)
    dealt = dealt.astype(BF16)
    long_own = fact(by_slot, 0, 2 * g) > 0.5
    sent = nt(dealt, p0_ref[...])
    wide_ref[...] = jnp.zeros_like(wide_ref)
    wide_ref[pl.ds(0, 64, stride=8), 0:16] = sent[0:64]
    wide_ref[pl.ds(1, 64, stride=8), 0:16] = sent[64:128]
    pbuf[...] = wide_ref[0:512, :].astype(BF16).reshape(64, 8, 128)
    pgot[g] = pbuf[g]

    to_mate(0).wait_recv()
    pg[t, 0:HALF, :] = jnp.where(long_own, part_ref[pl.ds(mine, HALF), :], pin[...])
    give(0)
    for j in range(4):
        to_mate(1 + j).wait_recv()
        rows = pl.ds(j * PIECE, PIECE)
        xg[t, rows, :] = jnp.where(long_own, xv_ref[pl.ds(mine + j * PIECE, PIECE), :], xin[rows, :])
        give(1 + j)
    to_mate(5).start()
    to_mate(6).start()
    pl.semaphore_wait(round1, 4)
    pass_on(round2, g, t, (3, 4, 5))

    hand_on(0)
    far_item(0)

    def low_rank(r0, n):
        parts = [pg[k, r0 : r0 + n, :].astype(F32) for k in range(TP)]
        return jnp.tanh(parts[0] + parts[1] + parts[2] + parts[3]).astype(BF16)

    lh[...] = low_rank(0, HALF)
    to_mate(9).start()
    lt_ref[pl.ds(mine, HALF), :] = lh[...]
    pl.semaphore_wait(round2, 3)
    scatter_rep(pbuf, pgot, p_send, p_recv, g, t)
    hand_on(1)

    for c in range(8):
        rows = mm(dealt, km_ref[pl.ds(c, 128, stride=8), :].astype(BF16))
        wide_ref[pl.ds(c, 64, stride=16), :] = rows[0:64]
        wide_ref[pl.ds(8 + c, 64, stride=16), :] = rows[64:128]
    sbuf[...] = wide_ref[...].astype(BF16).reshape(64, 16, 128)
    sgot[g] = sbuf[g]
    scatter_rep(sbuf, sgot, st_send, st_recv, g, t)
    hand_on(2)

    same = iota((128, 128), 0) // SPAN == iota((128, 128), 1) // SPAN
    heads_sum = same.astype(BF16)
    anchor, boost, scale, shift = anchor_ref[...], boost_ref[...], scale_ref[...], shift_ref[...]

    def ready(i, _):
        rows = pl.ds(pl.multiple_of(i * CHUNK, 16), CHUNK)
        log = -jnp.exp(anchor_ref[:, cols] + mm(lt_ref[rows, :], ex_ref[:, cols]))
        r = jnp.where(long_own, rown[rows, :], rmate[rows, :]).astype(F32)
        k = jnp.where(long_own, kown[rows, :], kmate[rows, :]).astype(F32)
        incl = running(log, CHUNK)
        q, kk, ri = scaled(r, k, incl, log, CHUNK)
        ri_ref[rows, :] = ri
        last = incl[CHUNK - 1 : CHUNK]
        kd = k * jnp.exp(last - incl)
        keep = jnp.exp(last)
        gain = mm(stack((r * boost_ref[:, cols] * k).astype(BF16), SPLIT), heads_sum)
        for p in range(SPLIT):
            c = lanes(p)
            gain_ref[rows, c] = gain[CHUNK * p : CHUNK * p + CHUNK]
            sc_ref[SPLIT * i + p] = scored(q[:, c], kk[:, c], CHUNK)
            kd_ref[SPLIT * i + p] = kd[:, c].T.astype(BF16)
            keep_ref[SPLIT * i + p] = column(keep[:, c])
        return 0

    def product(source, add):
        def tile(n, _):
            c = pl.ds(pl.multiple_of(n * 256, 256), 256)
            out = mm(xg[source], w_ref[pl.ds(pl.multiple_of(source * WID, WID), WID), c])
            acc[:, c] = acc[:, c] + out if add else out
            return 0

        lax.fori_loop(0, WID // 256, tile, 0, unroll=4)

    to_mate(5).wait_recv()
    to_mate(6).wait_recv()
    to_mate(9).wait_recv()

    spread = (iota((128, WID), 1) // SPAN == iota((128, WID), 0)).astype(BF16)
    own_lane = iota((64, WID), 1) % SPAN == iota((64, WID), 0)
    row16 = iota((16, WID), 0)
    firsts = []

    def late_rows():
        wait_rep(pgot, p_recv)
        wide_ref[0:512, :] = pgot[...].reshape(512, 128).astype(F32)
        before = []
        for s in range(2):
            vals = mm(wide_ref[pl.ds(s, 64, stride=8), :].astype(BF16), spread)
            before.append(jnp.sum(jnp.where(own_lane, vals, 0.0), axis=0, keepdims=True))
        final = x_ref[TAIL - 16 : TAIL, :].astype(F32)[15:16]
        firsts.extend([jnp.where(long_own, final, before[0]), before[1]])
        cur = [x_ref[0:16, :].astype(F32), gx_ref[0:16, :].astype(F32), gx_ref[16:32, :].astype(F32)]
        ahead = [jnp.where(row16 == 0, f, pltpu.roll(x, 1, 0)) for x, f in zip(cur, before[:1] + firsts)]
        zsend[...] = mixed(cur[0], ahead[0], mc).astype(BF16)
        zpart[...] = mm(mixed(cur[0], ahead[0], mf).astype(BF16), sh_ref[...]).astype(BF16)
        to_mate(7).start()
        to_mate(8).start()
        for s in range(2):
            at = HALF + 16 * s
            xg[t, at : at + 16, :] = mixed(cur[1 + s], ahead[1 + s], mc).astype(BF16)
            pg[t, at : at + 16, :] = mm(mixed(cur[1 + s], ahead[1 + s], mf).astype(BF16), sh_ref[...]).astype(BF16)

    def give_late():
        to_mate(7).wait_recv()
        to_mate(8).wait_recv()
        at = HALF + 32
        pg[t, at : at + 16, :] = jnp.where(long_own, zpart[...], zpin[...])
        first_rows = jnp.where(long_own, zsend[...], zin[...])
        xg[t, 0:16, :] = jnp.where(core == 0, first_rows, xg[t, 0:16, :])
        for item in (7, 5, 6):
            give(item)

    counts = []

    def edges_out():
        wide_ref[0:512, :] = jnp.zeros((512, 128), F32)
        for s in range(2):
            count = fact(by_slot, 1, 2 * g + s).astype(jnp.int32)
            counts.append(count)
            rows = gx_ref[DRAFT * s : DRAFT * s + DRAFT, :].astype(F32)
            edge = jnp.sum(jnp.where(row16 == count - 1, rows, 0.0), axis=0, keepdims=True)
            edge = jnp.where(count > 0, edge, firsts[s])
            wide_ref[pl.ds(s, 64, stride=8), :] = nt(jnp.where(own_lane, edge, 0.0).astype(BF16), spread)
        ebuf[...] = wide_ref[0:512, :].astype(BF16).reshape(64, 8, 128)
        egot[g] = ebuf[g]
        scatter_rep(ebuf, egot, e_send, e_recv, g, t)

    def draft_ready(s):
        rows = slice(DRAFT * s, DRAFT * s + DRAFT)
        log = -jnp.exp(anchor + mm(ll_ref[rows, :], ex_ref[...]))
        r, k = gr_ref[rows, :].astype(F32), gk_ref[rows, :].astype(F32)
        incl = running(log, DRAFT)
        q, kk, ri = scaled(r, k, incl, log, DRAFT)
        dri_ref[rows, :] = ri
        gain = mm(stack((r * boost * k).astype(BF16), PAIRS), heads_sum)
        taken = row16 < counts[s]
        upto = jnp.sum(jnp.where(taken, log, 0.0), axis=0, keepdims=True)
        weight = jnp.where(taken, jnp.exp(jnp.where(taken, upto - incl, 0.0)), 0.0)
        dkd_ref[rows, :] = (k * weight).astype(BF16)
        keep = jnp.exp(upto)
        dy_ref[s] = gain
        for p in range(PAIRS):
            c = lanes(p)
            dsc_ref[PAIRS * s + p] = scored(q[:, c], kk[:, c], DRAFT)
            dk_ref[s, p] = column(keep[:, c])

    def draft_values(s):
        rows = slice(DRAFT * s, DRAFT * s + DRAFT)
        low16 = iota((DRAFT, 128), 1) < SPAN
        for p in range(PAIRS):
            c = lanes(p)
            at = slice(DRAFT * p, DRAFT * p + DRAFT)
            v = vl_ref[rows, c]
            both = mm(dsc_ref[PAIRS * s + p], v)
            inner = jnp.where(low16, both[0:DRAFT], both[DRAFT : 2 * DRAFT])
            dy_ref[s, at, :] = inner + dy_ref[s, at, :] * v.astype(F32)
            du_ref[s, p] = jnp.where(same, tn(dkd_ref[rows, c], v), 0.0)

    lax.fori_loop(1, 4, ready, 0, unroll=3)
    hand_on(3)
    late_rows()
    lax.fori_loop(4, 6, ready, 0, unroll=2)
    give_late()
    hand_on(4)
    lax.fori_loop(6, 9, ready, 0, unroll=3)
    edges_out()
    for k in range(TP):
        w_copy(k).wait()
    product(t, False)
    hand_on(7)
    hand_on(5)
    hand_on(6)
    far_item(7)
    ll_ref[...] = low_rank(HALF, LATE)
    to_mate(14).start()
    product(left, True)
    wait_rep(sgot, st_recv)
    wide_ref[...] = sgot[...].reshape(1024, 128).astype(F32)
    for p in range(PAIRS):
        st0_ref[p] = wide_ref[pl.ds(p, 64, stride=16), :].astype(BF16)
    to_mate(11).start()
    for p in range(PAIRS):
        dk_ref[2, p] = halves(wide_ref[pl.ds(8 + p, 64, stride=16), :])
    lax.fori_loop(9, STEPS, ready, 0, unroll=3)
    to_mate(14).wait_recv()
    head = jnp.where(core == 0, ll_ref[32:33, :], lz_ref[0:1, :])
    lt_ref[0:16, :] = jnp.where(iota((16, RANK), 0) == 0, head, lt_ref[0:16, :])
    ready(0, 0)
    product(right, True)
    to_mate(11).wait_recv()
    for p in range(SPLIT):
        start = jnp.where(long_own, st0_ref[core * SPLIT + p], stm_ref[p])
        st_ref[p] = halves(start.astype(F32))
    for s in range(2):
        draft_ready(s)
    for item in range(1, 7):
        far_item(item)
    product(far, True)
    vh[...] = acc[0:HALF, :].astype(BF16)
    to_mate(10).start()
    vl_ref[...] = acc[HALF:ROWS, :].astype(BF16)
    vt_ref[pl.ds(mine, HALF), :] = vh[:, cols]

    def accept(s, p, state):
        rows = slice(DRAFT * s, DRAFT * s + DRAFT)
        at = slice(DRAFT * p, DRAFT * p + DRAFT)
        dy_ref[s, at, :] = dy_ref[s, at, :] + mm(dri_ref[rows, lanes(p)], state.astype(BF16))
        end = state * dk_ref[s, p] + du_ref[s, p]
        wide_ref[pl.ds(512 * s + p, 64, stride=8), :] = end[0:64] + end[64:128]

    def give_back(s):
        rbuf[s] = wide_ref[512 * s : 512 * s + 512, :].astype(BF16).reshape(64, 8, 128)
        rgot[s, g] = rbuf[s, g]
        scatter_rep(rbuf.at[s], rgot.at[s], b_send.at[s], b_recv.at[s], g, t)

    draft_values(1)
    for p in range(PAIRS):
        accept(1, p, dk_ref[2, p])
    give_back(1)

    to_mate(10).wait_recv()
    low32 = iota((CHUNK, 128), 1) < SPAN

    def step(i, _):
        rows = pl.ds(pl.multiple_of(i * CHUNK, 16), CHUNK)
        for p in range(SPLIT):
            c = lanes(p)
            v = vt_ref[rows, c]
            both = mm(sc_ref[SPLIT * i + p], v)
            state = st_ref[p]
            y = jnp.where(low32, both[0:CHUNK], both[CHUNK : 2 * CHUNK])
            y_ref[rows, c] = y + mm(ri_ref[rows, c], state.astype(BF16)) + gain_ref[rows, c] * v.astype(F32)
            st_ref[p] = state * keep_ref[SPLIT * i + p] + jnp.where(same, mm(kd_ref[SPLIT * i + p], v), 0.0)
        return 0

    lax.fori_loop(0, STEPS, step, 0, unroll=6)
    to_mate(12).start()

    draft_values(0)

    def finish(i, _):
        rows = pl.ds(pl.multiple_of(i * CHUNK, 16), CHUNK)
        y = stack(y_ref[rows, :], SPLIT)
        o_ref[rows, :] = normed(y, heads_sum, scale_ref[:, cols], shift_ref[:, cols], CHUNK, SPLIT).astype(BF16)
        return 0

    lax.fori_loop(0, STEPS // 2, finish, 0, unroll=2)
    to_mate(12).wait_recv()
    for p in range(PAIRS):
        end = jnp.where(core == p // SPLIT, st_ref[p % SPLIT], endm_ref[p % SPLIT])
        accept(0, p, jnp.where(long_own, end, halves(st0_ref[p].astype(F32))))
    give_back(0)
    lax.fori_loop(STEPS // 2, STEPS, finish, 0, unroll=2)
    to_mate(13).start()
    for s in range(2):
        draft_ref[DRAFT * s : DRAFT * s + DRAFT, :] = normed(
            dy_ref[s], heads_sum, scale, shift, DRAFT, PAIRS
        ).astype(BF16)
    tail_ref[:, cols] = jnp.where(long_own, o_ref[...], jnp.zeros((TAIL, SIDE), BF16))

    wait_rep(egot, e_recv)
    wide_ref[0:512, :] = egot[...].reshape(512, 128).astype(F32)
    edges = jnp.concatenate([wide_ref[pl.ds(0, 64, stride=8), :], wide_ref[pl.ds(1, 64, stride=8), :]], axis=0)
    prior_ref[...] = tn(edges.astype(BF16), dealt)[0:16].astype(BF16)
    to_mate(13).wait_recv()
    tail_ref[:, mate_cols] = jnp.where(long_own, om_ref[...], jnp.zeros((TAIL, SIDE), BF16))
    req_ref[...] = by_req
    outs = ((tail_ref, tail_hbm), (draft_ref, draft_hbm), (prior_ref, prior_hbm), (req_ref, req_hbm))
    puts = [pltpu.make_async_copy(a, b, out_sem.at[i]) for i, (a, b) in enumerate(outs)]
    for put in puts:
        put.start()
    for s in range(2):
        wait_rep(rgot.at[s], b_recv.at[s])
    for put in puts:
        put.wait()

    wait_rep(pbuf, p_send)
    wait_rep(sbuf, st_send)
    wait_rep(ebuf, e_send)
    for s in range(2):
        wait_rep(rbuf.at[s], b_send.at[s])
    for j in range(15):
        to_mate(j).wait_send()
    for item in range(8):
        move(item, t, right, right_send, left_recv).wait_send()
        move(item, t, left, left_send, right_recv).wait_send()
        move(item, far, right, hop_send, hop_recv).wait_send()


def place_kernel(
    tail_in, draft_in, back_in, prior_in, req_in, tail_out, draft_out, state_out, prior_out,
    tail, draft, back, prior, req, wide, state, get_sem, put_sem,
):
    src, mid = (back_in, req_in, tail_in, draft_in, prior_in), (back, req, tail, draft, prior)
    gets = [pltpu.make_async_copy(a, b, get_sem.at[i]) for i, (a, b) in enumerate(zip(src, mid))]
    outs = ((tail, tail_out), (draft, draft_out), (prior, prior_out), (state, state_out))
    puts = [pltpu.make_async_copy(a, b, put_sem.at[i]) for i, (a, b) in enumerate(outs)]
    for get in gets:
        get.start()
    gets[0].wait()
    gets[1].wait()
    wide[...] = back[...].reshape(1024, 128).astype(F32)
    for i in range(3):
        gets[2 + i].wait()
        puts[i].start()
    for c in range(8):
        rows = jnp.concatenate(
            [wide[pl.ds(c, 64, stride=8), :], wide[pl.ds(512 + c, 64, stride=8), :]], axis=0
        )
        state[pl.ds(c, 128, stride=8), :] = mm(req[...], rows.astype(BF16))
    puts[3].start()
    for put in puts:
        put.wait()


VM = pl.BlockSpec(memory_space=pltpu.VMEM)
ANY = pl.BlockSpec(memory_space=pl.ANY)
DMA = pltpu.SemaphoreType.DMA


def local(
    suffix_source, suffix_accept, suffix_address, guess_lane_source, guess_lane_accept, guess_lane_address,
    content_map, forget_shrink_map, forget_expand_map, forget_lane_anchor, present_boost,
    content_blend_share, forget_blend_share, lane_normal_scale, lane_normal_shift,
    kernel_memory_saved, prior_source_saved, lane_owner, request_spans, admitted_guesses,
):
    small = [a.reshape(1, 128) for a in (lane_owner, request_spans, admitted_guesses)]
    chan = [
        a.reshape(1, WID)
        for a in (forget_lane_anchor, present_boost, lane_normal_scale, lane_normal_shift)
    ]
    sds = jax.ShapeDtypeStruct
    shapes = (
        sds((TAIL, WID), BF16),
        sds((2 * DRAFT, WID), BF16),
        sds((1024, 128), F32),
        sds((16, 128), BF16),
    )
    vm = pltpu.VMEM
    row, ints, drafts = vm((1, WID), F32), vm((1, 128), jnp.int32), vm((2 * DRAFT, WID), BF16)
    side, tile16, tile8 = vm((TAIL, SIDE), BF16), vm((REP, 16, 128), BF16), vm((REP, 8, 128), BF16)
    outs = pl.pallas_call(
        mix_kernel,
        name="time_mix",
        out_shape=(shapes[0], shapes[1], sds((2, REP, 8, 128), BF16), shapes[3], sds((128, 128), BF16)),
        in_specs=[ANY] * 20,
        out_specs=(ANY, ANY, VM, ANY, ANY),
        scratch_shapes=[
            vm((TAIL, WID), BF16), drafts, vm((1024, 128), F32), vm((16, 128), BF16), row, row,
            ints, ints, ints, drafts, drafts, vm((RANK, WID), BF16), row, row, row, row,
            vm((TP * WID, WID), BF16), vm((WID, RANK), BF16), side, side,
            vm((128, 128), F32), vm((1024, 128), F32), tile16, tile16, tile8, tile8,
            vm((TAIL, WID), BF16), vm((TAIL, RANK), BF16), vm((HALF, WID), BF16), vm((HALF, RANK), BF16),
            vm((16, WID), BF16), vm((16, RANK), BF16), vm((16, WID), BF16), vm((16, RANK), BF16),
            vm((TP, ROWS, WID), BF16), vm((TP, HALF + LATE, RANK), BF16), vm((ROWS, WID), F32),
            vm((HALF, WID), BF16), vm((HALF, RANK), BF16), vm((32, WID), BF16), vm((LATE, RANK), BF16),
            side, vm((TAIL, RANK), BF16), side, side,
            vm((PAIRS, 64, 128), BF16), vm((SPLIT, 64, 128), BF16),
            vm((STEPS * SPLIT, 2 * CHUNK, CHUNK), BF16), side, vm((TAIL, SIDE), F32),
            vm((STEPS * SPLIT, 128, CHUNK), BF16), vm((STEPS * SPLIT, 128, 128), F32),
            vm((SPLIT, 128, 128), F32), vm((SPLIT, 128, 128), F32), vm((TAIL, SIDE), F32), side, side,
            vm((2, 128, 128), F32), drafts, vm((2, PAIRS, 128, 128), F32), vm((3, PAIRS, 128, 128), F32),
            vm((2, REP, 8, 128), BF16), tile8, tile8, vm((16, RANK), BF16),
            drafts, vm((2 * PAIRS, 2 * DRAFT, DRAFT), BF16), vm((TAIL, WID), BF16), drafts, vm((16, 128), BF16),
            vm((128, 128), BF16), DMA((4,)),
            DMA((19,)), DMA((TP,)), DMA, DMA, DMA, DMA, DMA, DMA, DMA((2,)), DMA((2,)), DMA((15,)), DMA((15,)),
            DMA((8,)), DMA((8,)), DMA((8,)), DMA((8,)), DMA((8,)), DMA((8,)),
            pltpu.SemaphoreType.REGULAR, pltpu.SemaphoreType.REGULAR,
        ],
        compiler_params=pltpu.CompilerParams(
            collective_id=0, has_side_effects=True, vmem_limit_bytes=56 << 20
        ),
    )(
        suffix_source.reshape(TAIL, WID),
        guess_lane_source.reshape(2 * DRAFT, WID),
        kernel_memory_saved.reshape(1024, 128),
        prior_source_saved.reshape(128, 16).T,
        content_blend_share.reshape(1, WID),
        forget_blend_share.reshape(1, WID),
        *small,
        guess_lane_accept.reshape(2 * DRAFT, WID),
        guess_lane_address.reshape(2 * DRAFT, WID),
        forget_expand_map,
        *chan,
        content_map,
        forget_shrink_map,
        suffix_accept.reshape(TAIL, WID),
        suffix_address.reshape(TAIL, WID),
    )
    tail, draft, state, prior = pl.pallas_call(
        place_kernel,
        name="place",
        out_shape=shapes,
        in_specs=[ANY] * 5,
        out_specs=(ANY,) * 4,
        scratch_shapes=[
            vm((TAIL, WID), BF16), drafts, vm((2, REP, 8, 128), BF16), vm((16, 128), BF16),
            vm((128, 128), BF16), vm((1024, 128), F32), vm((1024, 128), F32), DMA((5,)), DMA((4,)),
        ],
    )(*outs)
    return (
        tail.reshape(1, TAIL, WID),
        draft.reshape(2, DRAFT, WID),
        state.reshape(128, 1, WID),
        prior.T.reshape(128, 1, 16),
    )


def solution(mesh):
    rows, cols, chan = P("rep", None, "tp"), P(None, "tp"), P("tp")
    cache = P(None, "rep", "tp")
    return jax.shard_map(
        local,
        mesh=mesh,
        in_specs=(rows,) * 6 + (cols, P(), cols) + (chan,) * 6 + (cache, cache, P(), P(), P()),
        out_specs=(rows, rows, cache, cache),
        check_vma=False,
    )
```
